512 devices in a mesh: step: 16 (over z), band: 32 (over x, y, core).
Axes of the slice: x: 4, y: 4, z: 16, core: 2. Of those that a mesh axis runs over, the one named last changes fastest.
Arguments:
- states: float32 [16, 64, 10752], P('step', 'band'), may hold values from -6 to 6
- anchor: float32 [64, 10752], P('band'), may hold values from -6 to 6
- step_index: int32 [16], P('step'), may hold values from 0 to 19
- sigmas: float32 [20], replicated, may hold values from 0.05 to 0.5
- enc_w: bfloat16 [84, 512], replicated, may hold values from -0.625 to 0.625
- noise_embed: float32 [512], replicated, may hold values from -3 to 3
- qkv_w: bfloat16 [512, 1536], replicated, may hold values from -0.25 to 0.25
- out_w: bfloat16 [512, 512], replicated, may hold values from -0.25 to 0.25
- up_w: bfloat16 [512, 1024], replicated, may hold values from -0.25 to 0.25
- down_w: bfloat16 [1024, 512], replicated, may hold values from -0.1875 to 0.1875
- dec_w: bfloat16 [512, 84], replicated, may hold values from -0.25 to 0.25
Outputs:
- new_states: float32 [16, 64, 10752], P('step', 'band')
- change: float32 [16], P('step')
The draws below stay inside these ranges and needn't reach their ends.
All inputs are finite; a program needn't handle non-finite values.
Results may differ from the reference program's by a relative error of at most 0.0031.
Values may be sent and summed in bfloat16 or wider, within the bound.
No kernel may reach another device: no remote copies, remote signals or barrier semaphores. Data moves between devices by JAX's collectives and lax.ppermute only.
A program may use at most 64 MiB of HBM per device.

```python
import math
import jax
import jax.numpy as jnp
from jax import lax

LAT_DEV = 2
LON = 128
C = 84
W = 512
HEADS = 4
HEAD_DIM = 128
MLP = 1024
LEVELS = 20
R = 2
STEPS = 16
NLAT = 64


def plant(result, stream_key, least, high):
    longest = result.shape.index(max(result.shape))
    spots = []
    for shift in (0, 1):
        where = [jax.random.randint(jax.random.fold_in(stream_key, axis), (), 0, length) for axis, length in enumerate(result.shape)]
        where[longest] = (where[longest] + shift) % result.shape[longest]
        spots.append(tuple(where))
    return result.at[spots[0]].set(least).at[spots[1]].set(high)


def block_scale(own_key, shape, split, smallest, largest):
    level, own = 1.0, jax.random.fold_in(own_key, 6)
    for dim, shards_of in split:
        heights = jnp.exp(jax.random.uniform(jax.random.fold_in(own, dim), (shards_of,), jnp.float32, smallest / len(split), largest / len(split)))
        level = level * jnp.repeat(heights, shape[dim] // shards_of).reshape([-1 if axis == dim else 1 for axis in range(len(shape))])
    return level


def bell_draw(rng, shape, width, bound, pieces=(), held_as=jnp.bfloat16):
    array = width * jax.random.normal(rng, shape, jnp.float32)
    if pieces:
        array = array * block_scale(rng, shape, pieces, -0.22, 0.18)
    return jnp.clip(array, -bound, bound).astype(held_as)


def setup_inputs(seed: int = 0) -> dict:
    keys = jax.random.split(jax.random.key(seed), 12)
    states = bell_draw(keys[0], (STEPS, NLAT, LON * C), 1.0, 6.0, ((0, 16), (1, 32)), jnp.float32)
    anchor = bell_draw(keys[1], (NLAT, LON * C), 1.0, 6.0, ((0, 32),), jnp.float32)
    step_index = plant(jax.random.randint(keys[2], (STEPS,), 0, LEVELS), jax.random.fold_in(keys[2], 1), 0, LEVELS - 1).astype(jnp.int32)
    sigmas = jnp.clip(jnp.exp(jax.random.uniform(keys[3], (LEVELS,), jnp.float32, math.log(0.05), math.log(0.5))), 0.05, 0.5)
    enc_w = bell_draw(keys[4], (C, W), C ** -0.5, 0.625)
    noise_embed = bell_draw(keys[5], (W,), 0.5, 3.0, (), jnp.float32)
    qkv_w = bell_draw(keys[6], (W, 3 * W), W ** -0.5, 0.25)
    out_w = bell_draw(keys[7], (W, W), W ** -0.5, 0.25)
    up_w = bell_draw(keys[8], (W, MLP), W ** -0.5, 0.25)
    down_w = bell_draw(keys[9], (MLP, W), MLP ** -0.5, 0.1875)
    dec_w = bell_draw(keys[10], (W, C), W ** -0.5, 0.25)
    return {"states": states, "anchor": anchor, "step_index": step_index, "sigmas": sigmas, "enc_w": enc_w, "noise_embed": noise_embed, "qkv_w": qkv_w, "out_w": out_w, "up_w": up_w, "down_w": down_w, "dec_w": dec_w}


epsilon = 1e-06
score_gain = 3.0

def rms_scale(values):
    return values * lax.rsqrt(lax.optimization_barrier(jnp.mean(values * values, axis=-1, keepdims=True)) + epsilon)

def split_heads(projected):
    heads = rms_scale(projected.reshape(projected.shape[0], HEADS, HEAD_DIM))
    return heads.astype(jnp.bfloat16)

def window_mask_for(first_row, lat_rows, total_rows):
    offsets = jnp.arange(lat_rows + 2 * R, dtype=jnp.int32) - R
    key_rows = first_row + offsets
    inside = (key_rows >= 0) & (key_rows < total_rows)
    near = jnp.abs(jnp.arange(lat_rows, dtype=jnp.int32)[:, None] - offsets[None, :]) <= R
    return (inside[None, :] & near).astype(jnp.float32)

def attend(queries, key_heads, value_heads, window_mask):
    scores = jnp.einsum('qhd,khd->hqk', queries.astype(jnp.float32), key_heads.astype(jnp.float32))
    scores = scores * (score_gain / math.sqrt(HEAD_DIM))
    heads, count_q, count_k = scores.shape
    rows_q = window_mask.shape[0]
    rows_k = window_mask.shape[1]
    columns = count_q // rows_q
    weights = jnp.exp(scores).reshape(heads, rows_q, columns, rows_k, columns)
    weights = (weights * window_mask[None, :, None, :, None]).reshape(heads, count_q, count_k)
    softmax_weights = (weights / lax.optimization_barrier(jnp.sum(weights, axis=-1, keepdims=True))).astype(jnp.bfloat16)
    attended = jnp.einsum('hqk,khd->qhd', softmax_weights.astype(jnp.float32), value_heads.astype(jnp.float32))
    return attended.astype(jnp.bfloat16).reshape(count_q, W)

def finish_block(embedded, attended, out_w, up_w, down_w, dec_w):
    mixed = embedded + jnp.dot(attended, out_w, preferred_element_type=jnp.float32)
    normed = rms_scale(mixed).astype(jnp.bfloat16)
    hidden = jax.nn.gelu(jnp.dot(normed, up_w, preferred_element_type=jnp.float32)).astype(jnp.bfloat16)
    mixed = mixed + jnp.dot(hidden, down_w, preferred_element_type=jnp.float32)
    return jnp.dot(rms_scale(mixed).astype(jnp.bfloat16), dec_w, preferred_element_type=jnp.float32)

def step_drift(fields, noise_level, enc_w, noise_embed, qkv_w, out_w, up_w, down_w, dec_w):
    columns = fields.shape[1] // C
    tokens = fields.astype(jnp.bfloat16).reshape(-1, C)
    embedded = jnp.dot(tokens, enc_w, preferred_element_type=jnp.float32) + (jnp.log(noise_level) * noise_embed)[None, :]
    normed = rms_scale(embedded).astype(jnp.bfloat16)
    projected = jnp.dot(normed, qkv_w, preferred_element_type=jnp.float32)
    queries = split_heads(projected[:, :W]).reshape(NLAT, columns, HEADS, HEAD_DIM)
    key_heads = split_heads(projected[:, W:2 * W]).reshape(NLAT, columns, HEADS, HEAD_DIM)
    value_heads = projected[:, 2 * W:].astype(jnp.bfloat16).reshape(NLAT, columns, HEADS, HEAD_DIM)
    padding = ((R, R), (0, 0), (0, 0), (0, 0))
    key_grid = jnp.pad(key_heads, padding)
    value_grid = jnp.pad(value_heads, padding)
    embed_grid = embedded.reshape(NLAT, columns, W)

    def one_band(band):
        first_row = (band * LAT_DEV).astype(jnp.int32)
        band_queries = lax.dynamic_slice_in_dim(queries, first_row, LAT_DEV, 0).reshape(-1, HEADS, HEAD_DIM)
        band_keys = lax.dynamic_slice_in_dim(key_grid, first_row, LAT_DEV + 2 * R, 0).reshape(-1, HEADS, HEAD_DIM)
        band_values = lax.dynamic_slice_in_dim(value_grid, first_row, LAT_DEV + 2 * R, 0).reshape(-1, HEADS, HEAD_DIM)
        band_embed = lax.dynamic_slice_in_dim(embed_grid, first_row, LAT_DEV, 0).reshape(-1, W)
        window_mask = window_mask_for(first_row, LAT_DEV, NLAT)
        attended = attend(band_queries, band_keys, band_values, window_mask)
        drift_rows = finish_block(band_embed, attended, out_w, up_w, down_w, dec_w)
        return drift_rows.reshape(LAT_DEV, columns * C)
    drifts = lax.map(one_band, jnp.arange(NLAT // LAT_DEV, dtype=jnp.int32))
    return drifts.reshape(NLAT, columns * C)

def reference(states, anchor, step_index, sigmas, enc_w, noise_embed, qkv_w, out_w, up_w, down_w, dec_w):
    inputs = jnp.concatenate([anchor[None], states[:-1]], axis=0)
    noise_levels = sigmas[step_index]

    def one_step(packed):
        fields, noise_level = packed
        return step_drift(fields, noise_level, enc_w, noise_embed, qkv_w, out_w, up_w, down_w, dec_w)
    drifts = lax.map(one_step, (inputs, noise_levels))
    new_states = anchor[None] + jnp.cumsum(noise_levels[:, None, None] * drifts, axis=0)
    latitude = jnp.pi * ((jnp.arange(NLAT, dtype=jnp.float32) + 0.5) / NLAT - 0.5)
    area = jnp.cos(latitude)
    mismatch = new_states - states
    change = lax.optimization_barrier(jnp.sum(area[None, :, None] * mismatch * mismatch, axis=(1, 2))) / (jnp.sum(area) * (LON * C))
    return (new_states, change)
```

```python
import math

import jax
import jax.numpy as jnp
import numpy as np
from jax import lax
from jax.experimental import pallas as pl
from jax.experimental.pallas import tpu as pltpu
from jax.sharding import PartitionSpec as P

C = 84
W = 512
HEADS = 4
HEAD_DIM = 128
MLP = 1024
LON = 128
NLAT = 64
LANES = 128
GROUP = 32
SPAN = GROUP * C
PACKS = LON // GROUP
SUB = 2 * PACKS
TILES = SPAN // LANES
TOK = 2 * LON

epsilon = 1e-06
SCORE = 3.0 / math.sqrt(HEAD_DIM)

F32 = jnp.float32
BF16 = jnp.bfloat16


def rms(v):
    return v * lax.rsqrt(jnp.mean(v * v, axis=-1, keepdims=True) + epsilon)


def mm(a, b):
    return jnp.dot(a, b, preferred_element_type=F32)


def to_packed(rows):
    return jnp.concatenate([rows[:, g * SPAN : (g + 1) * SPAN] for g in range(PACKS)], axis=0)


def open_kernel(states_ref, anchor_ref, out_ref):
    last = lax.axis_index("step") == lax.axis_size("step") - 1

    @pl.when(last)
    def _():
        out_ref[...] = to_packed(anchor_ref[...]).astype(BF16)

    @pl.when(jnp.logical_not(last))
    def _():
        out_ref[...] = to_packed(states_ref[0]).astype(BF16)


def unpack_tokens(block_ref, tok_ref):
    lane = lax.broadcasted_iota(jnp.int32, (SUB, LANES), 1)
    x = block_ref[...].astype(F32)
    for r in range(GROUP):
        tile, off = divmod(r * C, LANES)
        v = x[:, tile * LANES : (tile + 1) * LANES]
        if off + C > LANES:
            v = jnp.where(lane >= off, v, x[:, (tile + 1) * LANES : (tile + 2) * LANES])
        if off:
            v = pltpu.roll(v, LANES - off, 1)
        tok_ref[r * SUB : (r + 1) * SUB, :] = v


def denoise_kernel(
    index_ref, sigma_ref, before_ref, here_ref, after_ref, enc_ref, embed_ref, qkv_ref, out_w_ref,
    up_ref, down_ref, dec_ref, drift_ref, drift16_ref, tok_ref,
):
    band = lax.axis_index("band")
    bands = lax.axis_size("band")
    noise = sigma_ref[index_ref[0]]
    offset = jnp.log(jnp.full((1, W), noise, F32)) * embed_ref[...]

    def embed(ref):
        unpack_tokens(ref, tok_ref)
        embedded = mm(tok_ref[...].astype(BF16), enc_ref[...]) + offset
        return embedded, rms(embedded).astype(BF16)

    def heads_of(projected):
        return [
            rms(projected[:, h * HEAD_DIM : (h + 1) * HEAD_DIM]).astype(BF16) for h in range(HEADS)
        ]

    embedded, normed = embed(here_ref)
    queries = heads_of(mm(normed, qkv_ref[:, :W]))
    blocks = [normed, embed(before_ref)[1], embed(after_ref)[1]]
    keys = [heads_of(mm(n, qkv_ref[:, W : 2 * W])) for n in blocks]
    values = [mm(n, qkv_ref[:, 2 * W :]).astype(BF16) for n in blocks]

    q_row = lax.broadcasted_iota(jnp.int32, (TOK, TOK), 0) % 2
    k_row = lax.broadcasted_iota(jnp.int32, (TOK, TOK), 1) % 2
    see_before = (((q_row == 0) | (k_row == 1)) & (band > 0)).astype(F32)
    see_after = (((q_row == 1) | (k_row == 0)) & (band < bands - 1)).astype(F32)
    masks = [None, see_before, see_after]

    attended = []
    for h in range(HEADS):
        total, mix = 0.0, 0.0
        for n in range(3):
            scores = lax.dot_general(
                queries[h], keys[n][h], (((1,), (1,)), ((), ())), preferred_element_type=F32
            )
            weights = jnp.exp(scores * SCORE)
            if masks[n] is not None:
                weights = weights * masks[n]
            total = total + jnp.sum(weights, axis=-1, keepdims=True)
            mix = mix + mm(weights.astype(BF16), values[n][:, h * HEAD_DIM : (h + 1) * HEAD_DIM])
        attended.append((mix / total).astype(BF16))
    attended = jnp.concatenate(attended, axis=1)

    mixed = embedded + mm(attended, out_w_ref[...])
    hidden = jax.nn.gelu(mm(rms(mixed).astype(BF16), up_ref[...])).astype(BF16)
    mixed = mixed + mm(hidden, down_ref[...])
    drift = mm(rms(mixed).astype(BF16), dec_ref[...]) * noise

    lane = lax.broadcasted_iota(jnp.int32, (SUB, LANES), 1)
    tiles = [0.0] * TILES
    for r in range(GROUP):
        tile, off = divmod(r * C, LANES)
        v = drift[r * SUB : (r + 1) * SUB, :]
        if off:
            v = pltpu.roll(v, off, 1)
        if off + C > LANES:
            tiles[tile] = tiles[tile] + jnp.where(lane >= off, v, 0.0)
            tiles[tile + 1] = tiles[tile + 1] + jnp.where(lane < off, v, 0.0)
        else:
            tiles[tile] = tiles[tile] + v
    packed = jnp.concatenate(tiles, axis=1)
    drift_ref[...] = packed
    drift16_ref[...] = packed.astype(BF16)


def close_kernel(area_ref, gathered_ref, drift_ref, anchor_ref, states_ref, new_ref, part_ref):
    step = lax.axis_index("step")
    band = lax.axis_index("band")

    def add(j, total):
        return total + gathered_ref[j].astype(F32)

    earlier = lax.fori_loop(0, step, add, jnp.zeros((SUB, SPAN), F32))
    change = earlier + drift_ref[...]
    row = lax.broadcasted_iota(jnp.int32, (2, 1), 0)
    area = jnp.where(row == 0, area_ref[2 * band], area_ref[2 * band + 1])
    part = jnp.zeros((2, LANES), F32)
    for g in range(PACKS):
        at = slice(g * SPAN, (g + 1) * SPAN)
        new = anchor_ref[:, at] + change[2 * g : 2 * g + 2, :]
        new_ref[0, :, at] = new
        miss = new - states_ref[0, :, at]
        miss = miss * miss
        for t in range(TILES):
            part = part + miss[:, t * LANES : (t + 1) * LANES]
    part = jnp.sum(part * area, axis=0, keepdims=True)
    part_ref[...] = jnp.broadcast_to(part, part_ref.shape)


def local(
    states, anchor, step_index, sigmas, enc_w, noise_embed, qkv_w, out_w, up_w, down_w, dec_w
):
    steps, bands = lax.axis_size("step"), lax.axis_size("band")
    vmem = pl.BlockSpec(memory_space=pltpu.VMEM)
    smem = pl.BlockSpec(memory_space=pltpu.SMEM)
    shape = jax.ShapeDtypeStruct

    block = pl.pallas_call(
        open_kernel, out_shape=shape((SUB, SPAN), BF16), in_specs=[vmem] * 2, out_specs=vmem,
        name="open",
    )(states, anchor)

    def shifted(by):
        pairs = [
            (s * bands + b, ((s + 1) % steps) * bands + b + by)
            for s in range(steps) for b in range(bands) if 0 <= b + by < bands
        ]
        return lax.ppermute(block, ("step", "band"), pairs)

    here, before, after = shifted(0), shifted(1), shifted(-1)
    enc = jnp.pad(enc_w, ((0, LANES - C), (0, 0)))
    dec = jnp.pad(dec_w, ((0, 0), (0, LANES - C)))
    drift, drift16 = pl.pallas_call(
        denoise_kernel,
        out_shape=(shape((SUB, SPAN), F32), shape((SUB, SPAN), BF16)),
        in_specs=[smem] * 2 + [vmem] * 10, out_specs=(vmem, vmem),
        scratch_shapes=[pltpu.VMEM((TOK, LANES), F32)],
        name="denoise",
    )(step_index, sigmas, before, here, after, enc, noise_embed[None], qkv_w, out_w, up_w, down_w, dec)

    gathered = lax.all_gather(drift16, "step")

    latitude = np.pi * ((np.arange(NLAT, dtype=np.float32) + 0.5) / NLAT - 0.5)
    area = np.cos(latitude).astype(np.float32)
    new_states, part = pl.pallas_call(
        close_kernel,
        out_shape=(shape(states.shape, F32), shape((bands, LANES), F32)),
        in_specs=[smem] + [vmem] * 4, out_specs=(vmem, vmem),
        name="close",
    )(jnp.asarray(area), gathered, drift, anchor, states)
    parts = lax.all_to_all(part, "band", 0, 0, tiled=True)
    change = jnp.sum(parts)[None] / (np.float32(area.sum()) * (LON * C))
    return new_states, change


def solution(mesh):
    placed = (
        P("step", "band", None), P("band", None), P("step"), P(), P(), P(), P(), P(), P(), P(), P(),
    )
    return jax.shard_map(
        local,
        mesh=mesh,
        in_specs=placed,
        out_specs=(P("step", "band", None), P("step")),
        check_vma=False,
    )
```

```python
import math

import jax
import jax.numpy as jnp
import numpy as np
from jax import lax
from jax.experimental import pallas as pl
from jax.experimental.pallas import tpu as pltpu
from jax.sharding import PartitionSpec as P

C = 84
W = 512
HEADS = 4
HEAD_DIM = 128
MLP = 1024
LON = 128
NLAT = 64
LEVELS = 20
LANES = 128
GROUP = 32
SPAN = GROUP * C
PACKS = LON // GROUP
SUB = 2 * PACKS
TILES = SPAN // LANES
TOK = 2 * LON

epsilon = 1e-06
SCORE = 3.0 / math.sqrt(HEAD_DIM)

F32 = jnp.float32
BF16 = jnp.bfloat16


def rms(v):
    return v * lax.rsqrt(jnp.mean(v * v, axis=-1, keepdims=True) + epsilon)


def mm(a, b):
    return jnp.dot(a, b, preferred_element_type=F32)


def to_packed(rows):
    return jnp.concatenate([rows[:, g * SPAN : (g + 1) * SPAN] for g in range(PACKS)], axis=0)


def open_kernel(states_ref, anchor_ref, out_ref, rows_ref):
    last = lax.axis_index("step") == lax.axis_size("step") - 1

    @pl.when(last)
    def _():
        pltpu.sync_copy(anchor_ref, rows_ref)

    @pl.when(jnp.logical_not(last))
    def _():
        pltpu.sync_copy(states_ref.at[0], rows_ref)

    out_ref[...] = to_packed(rows_ref[...]).astype(BF16)


def unpack_tokens(block_ref, tok_ref):
    lane = lax.broadcasted_iota(jnp.int32, (SUB, LANES), 1)
    x = block_ref[...].astype(F32)
    for r in range(GROUP):
        tile, off = divmod(r * C, LANES)
        v = x[:, tile * LANES : (tile + 1) * LANES]
        if off + C > LANES:
            v = jnp.where(lane >= off, v, x[:, (tile + 1) * LANES : (tile + 2) * LANES])
        if off:
            v = pltpu.roll(v, LANES - off, 1)
        tok_ref[r * SUB : (r + 1) * SUB, :] = v


def embed(ref, tok_ref, enc, offset):
    unpack_tokens(ref, tok_ref)
    embedded = mm(tok_ref[...].astype(BF16), enc) + offset
    return embedded, rms(embedded).astype(BF16)


def heads_of(projected):
    return jnp.concatenate(
        [rms(projected[:, h * HEAD_DIM : (h + 1) * HEAD_DIM]) for h in range(HEADS)], axis=1
    ).astype(BF16)


def denoise_kernel(
    noise_ref, here_ref, before_ref, after_ref, offset_ref, enc_hbm, qkv_hbm, out_w_hbm, up_hbm,
    down_hbm, dec_hbm, drift_ref, copies_ref, tok_ref, enc_ref, qkv_ref, out_w_ref, up_ref,
    down_ref, dec_ref, sems,
):
    pairs = (
        (enc_hbm, enc_ref), (qkv_hbm, qkv_ref), (out_w_hbm, out_w_ref), (up_hbm, up_ref),
        (down_hbm, down_ref), (dec_hbm, dec_ref),
    )
    loads = [pltpu.make_async_copy(a, b, sems.at[i]) for i, (a, b) in enumerate(pairs)]
    for load in loads:
        load.start()
    band = lax.axis_index("band")
    bands = lax.axis_size("band")
    noise = noise_ref[0]
    offset = offset_ref[...]

    loads[0].wait()
    enc = jnp.concatenate(
        [enc_ref[...].astype(F32), jnp.zeros((LANES - C, W), F32)], axis=0
    ).astype(BF16)
    embedded, normed = embed(here_ref, tok_ref, enc, offset)
    loads[1].wait()
    queries = heads_of(mm(normed, qkv_ref[:, :W]))
    blocks = [normed]
    blocks += [embed(ref, tok_ref, enc, offset)[1] for ref in (before_ref, after_ref)]
    keys = [heads_of(mm(n, qkv_ref[:, W : 2 * W])) for n in blocks]
    values = [mm(n, qkv_ref[:, 2 * W :]).astype(BF16) for n in blocks]

    q_row = lax.broadcasted_iota(jnp.int32, (TOK, TOK), 0) % 2
    k_row = lax.broadcasted_iota(jnp.int32, (TOK, TOK), 1) % 2
    see_before = (((q_row == 0) | (k_row == 1)) & (band > 0)).astype(F32)
    see_after = (((q_row == 1) | (k_row == 0)) & (band < bands - 1)).astype(F32)
    masks = [None, see_before, see_after]

    attended = []
    for h in range(HEADS):
        at = slice(h * HEAD_DIM, (h + 1) * HEAD_DIM)
        total, mix = 0.0, 0.0
        for n in range(3):
            scores = lax.dot_general(
                queries[:, at], keys[n][:, at], (((1,), (1,)), ((), ())),
                preferred_element_type=F32,
            )
            weights = jnp.exp(scores * SCORE)
            if masks[n] is not None:
                weights = weights * masks[n]
            total = total + jnp.sum(weights, axis=-1, keepdims=True)
            mix = mix + mm(weights.astype(BF16), values[n][:, at])
        attended.append((mix / total).astype(BF16))
    attended = jnp.concatenate(attended, axis=1)

    loads[2].wait()
    mixed = embedded + mm(attended, out_w_ref[...])
    loads[3].wait()
    hidden = jax.nn.gelu(mm(rms(mixed).astype(BF16), up_ref[...])).astype(BF16)
    loads[4].wait()
    mixed = mixed + mm(hidden, down_ref[...])
    loads[5].wait()
    last = rms(mixed).astype(BF16)
    dec = jnp.concatenate([dec_ref[...].astype(F32), jnp.zeros((LANES - C, W), F32)], axis=0)
    drift = noise * lax.dot_general(
        last, dec.astype(BF16), (((1,), (1,)), ((), ())), preferred_element_type=F32
    )

    lane = lax.broadcasted_iota(jnp.int32, (SUB, LANES), 1)
    tiles = [0.0] * TILES
    for r in range(GROUP):
        tile, off = divmod(r * C, LANES)
        v = drift[r * SUB : (r + 1) * SUB, :]
        if off:
            v = pltpu.roll(v, off, 1)
        if off + C > LANES:
            tiles[tile] = tiles[tile] + jnp.where(lane >= off, v, 0.0)
            tiles[tile + 1] = tiles[tile + 1] + jnp.where(lane < off, v, 0.0)
        else:
            tiles[tile] = tiles[tile] + v
    packed = jnp.concatenate(tiles, axis=1)
    drift_ref[...] = packed
    packed = packed.astype(BF16)
    for i in range(4):
        copies_ref[i] = packed


def middle_kernel(group_ref, drift_ref, sent_ref, window_ref):
    place = lax.axis_index("step") % 4
    parts = [group_ref[i].astype(F32) for i in range(4)]
    sent_ref[...] = ((parts[0] + parts[1]) + (parts[2] + parts[3])).astype(BF16)
    window = drift_ref[...]
    for i in range(3):
        window = window + jnp.where(place > i, parts[i], 0.0)
    window_ref[...] = window


def close_kernel(
    area_ref, sum_ref, back4_ref, back8_ref, back12_ref, anchor_ref, states_ref, new_ref, part_ref
):
    band = lax.axis_index("band")
    change = (
        sum_ref[...] + back4_ref[...].astype(F32) + back8_ref[...].astype(F32)
        + back12_ref[...].astype(F32)
    )
    row = lax.broadcasted_iota(jnp.int32, (2, 1), 0)
    area = jnp.where(row == 0, area_ref[2 * band], area_ref[2 * band + 1])
    part = jnp.zeros((2, LANES), F32)
    for g in range(PACKS):
        at = slice(g * SPAN, (g + 1) * SPAN)
        new = anchor_ref[:, at] + change[2 * g : 2 * g + 2, :]
        new_ref[0, :, at] = new
        miss = new - states_ref[0, :, at]
        miss = miss * miss
        for t in range(TILES):
            part = part + miss[:, t * LANES : (t + 1) * LANES]
    part = jnp.sum(part * area, axis=0, keepdims=True)
    part_ref[...] = jnp.broadcast_to(part, part_ref.shape)


def local_vmem(*arrays):
    return [pltpu.with_memory_space_constraint(a, pltpu.VMEM) for a in arrays]


def in_hbm(*arrays):
    return [pltpu.with_memory_space_constraint(a, pltpu.HBM) for a in arrays]


def local(
    states, anchor, step_index, sigmas, enc_w, noise_embed, qkv_w, out_w, up_w, down_w, dec_w
):
    steps, bands = lax.axis_size("step"), lax.axis_size("band")
    vmem = pl.BlockSpec(memory_space=pltpu.VMEM)
    smem = pl.BlockSpec(memory_space=pltpu.SMEM)
    hbm = pl.BlockSpec(memory_space=pltpu.HBM)
    shape = jax.ShapeDtypeStruct

    block = pl.pallas_call(
        open_kernel, out_shape=pltpu.VMEM((SUB, SPAN), BF16), in_specs=[hbm] * 2, out_specs=vmem,
        scratch_shapes=[pltpu.VMEM((2, LON * C), F32)],
        name="open", compiler_params=pltpu.CompilerParams(vmem_limit_bytes=8 << 20),
    )(*in_hbm(states, anchor))

    def later(array, by):
        return lax.ppermute(array, "step", [(s, s + by) for s in range(steps - by)])

    def shifted(by):
        pairs = [
            (s * bands + b, ((s + 1) % steps) * bands + b + by)
            for s in range(steps) for b in range(bands) if 0 <= b + by < bands
        ]
        return lax.ppermute(block, ("step", "band"), pairs)

    here, before, after = shifted(0), shifted(1), shifted(-1)
    onehot = step_index[:, None] == jnp.arange(LEVELS, dtype=jnp.int32)[None, :]
    noise = jnp.sum(jnp.where(onehot, sigmas[None, :], 0.0), axis=1)
    offset = jnp.log(noise)[:, None] * noise_embed[None, :]
    weights = (enc_w, qkv_w, out_w, up_w, down_w, dec_w.T)
    drift, copies = pl.pallas_call(
        denoise_kernel,
        out_shape=(pltpu.VMEM((SUB, SPAN), F32), pltpu.VMEM((4, SUB, SPAN), BF16)),
        in_specs=[smem] + [vmem] * 4 + [hbm] * 6, out_specs=(vmem, vmem),
        scratch_shapes=[pltpu.VMEM((TOK, LANES), F32)]
        + [pltpu.VMEM(w.shape, BF16) for w in weights]
        + [pltpu.SemaphoreType.DMA((len(weights),))],
        name="denoise", compiler_params=pltpu.CompilerParams(vmem_limit_bytes=32 << 20),
    )(noise, *local_vmem(here, before, after, offset), *in_hbm(*weights))

    group = lax.all_to_all(
        copies, "step", 0, 0, tiled=True,
        axis_index_groups=[[4 * g + i for i in range(4)] for g in range(steps // 4)],
    )
    sent, window = pl.pallas_call(
        middle_kernel, out_shape=(pltpu.VMEM((SUB, SPAN), BF16), pltpu.VMEM((SUB, SPAN), F32)),
        in_specs=[vmem] * 2, out_specs=(vmem, vmem), name="middle",
        compiler_params=pltpu.CompilerParams(vmem_limit_bytes=8 << 20),
    )(*local_vmem(group, drift))
    far = [later(sent, by) for by in (4, 8, 12)]

    latitude = np.pi * ((np.arange(NLAT, dtype=np.float32) + 0.5) / NLAT - 0.5)
    area = np.cos(latitude).astype(np.float32)
    new_states, part = pl.pallas_call(
        close_kernel,
        out_shape=(shape(states.shape, F32), pltpu.VMEM((bands, LANES), F32)),
        in_specs=[smem] + [vmem] * 6, out_specs=(vmem, vmem),
        name="close", compiler_params=pltpu.CompilerParams(vmem_limit_bytes=16 << 20),
    )(jnp.asarray(area), *local_vmem(window, *far, anchor, states))
    parts = lax.all_to_all(part, "band", 0, 0, tiled=True)
    change = jnp.sum(parts)[None] / (np.float32(area.sum()) * (LON * C))
    return new_states, change


def solution(mesh):
    placed = (
        P("step", "band", None), P("band", None), P("step"), P(), P(), P(), P(), P(), P(), P(), P(),
    )
    return jax.shard_map(
        local,
        mesh=mesh,
        in_specs=placed,
        out_specs=(P("step", "band", None), P("step")),
        check_vma=False,
    )
```

```python
import math

import jax
import jax.numpy as jnp
import numpy as np
from jax import lax
from jax.experimental import pallas as pl
from jax.experimental.pallas import tpu as pltpu
from jax.sharding import PartitionSpec as P

C = 84
W = 512
HEADS = 4
HEAD_DIM = 128
LON = 128
NLAT = 64
LEVELS = 20
LANES = 128
GROUP = 32
SPAN = GROUP * C
PACKS = LON // GROUP
SUB = 2 * PACKS
TILES = SPAN // LANES
TOK = 2 * LON

FAR = (
    [(2, 3), (0, 4), (1, 5), (15, 6)] + [(s, s + 4) for s in range(3, 11)] + [(14, 15)],
    [(2, 7), (1, 8), (0, 9), (15, 10), (6, 11), (5, 12), (4, 13), (3, 14), (10, 15)],
    [(15, 11), (0, 12), (1, 13), (2, 14), (3, 15)],
)

epsilon = 1e-06
SCORE = 3.0 / math.sqrt(HEAD_DIM)

F32 = jnp.float32
BF16 = jnp.bfloat16


def rms(v):
    return v * lax.rsqrt(jnp.mean(v * v, axis=-1, keepdims=True) + epsilon)


def mm(a, b):
    return jnp.dot(a, b, preferred_element_type=F32)


def to_packed(rows):
    return jnp.concatenate([rows[:, g * SPAN : (g + 1) * SPAN] for g in range(PACKS)], axis=0)


def open_kernel(states_ref, anchor_ref, out_ref, rows_ref):
    last = lax.axis_index("step") == lax.axis_size("step") - 1

    @pl.when(last)
    def _():
        pltpu.sync_copy(anchor_ref, rows_ref)

    @pl.when(jnp.logical_not(last))
    def _():
        pltpu.sync_copy(states_ref.at[0], rows_ref)

    out_ref[...] = to_packed(rows_ref[...]).astype(BF16)


def unpack_tokens(block_ref, tok_ref):
    lane = lax.broadcasted_iota(jnp.int32, (SUB, LANES), 1)
    x = block_ref[...].astype(F32)
    for r in range(GROUP):
        tile, off = divmod(r * C, LANES)
        v = x[:, tile * LANES : (tile + 1) * LANES]
        if off + C > LANES:
            v = jnp.where(lane >= off, v, x[:, (tile + 1) * LANES : (tile + 2) * LANES])
        if off:
            v = pltpu.roll(v, LANES - off, 1)
        tok_ref[r * SUB : (r + 1) * SUB, :] = v


def embed(ref, tok_ref, enc_ref, offset):
    unpack_tokens(ref, tok_ref)
    enc = jnp.concatenate(
        [enc_ref[...].astype(F32), jnp.zeros((LANES - C, W), F32)], axis=0
    ).astype(BF16)
    embedded = mm(tok_ref[...].astype(BF16), enc) + offset
    return embedded, rms(embedded).astype(BF16)


def heads_of(projected):
    return jnp.concatenate(
        [rms(projected[:, h * HEAD_DIM : (h + 1) * HEAD_DIM]) for h in range(HEADS)], axis=1
    ).astype(BF16)


def own_kernel(
    index_ref, sigma_ref, embed_ref, here_ref, enc_ref, qkv_ref, embedded_ref, heads_ref,
    offset_ref, noise_ref, tok_ref,
):
    level = lax.broadcasted_iota(jnp.int32, (1, LEVELS), 1)
    noise = jnp.sum(
        jnp.where(level == index_ref[...], sigma_ref[...], 0.0), axis=1, keepdims=True
    )
    offset = jnp.log(noise) * embed_ref[...]
    offset_ref[...] = offset
    noise_ref[...] = jnp.broadcast_to(noise, noise_ref.shape)
    embedded, normed = embed(here_ref, tok_ref, enc_ref, offset)
    embedded_ref[...] = embedded
    heads_ref[0] = heads_of(mm(normed, qkv_ref[:, :W]))
    heads_ref[1] = heads_of(mm(normed, qkv_ref[:, W : 2 * W]))
    heads_ref[2] = mm(normed, qkv_ref[:, 2 * W :]).astype(BF16)


def denoise_kernel(
    before_ref, after_ref, embedded_ref, heads_ref, offset_ref, noise_ref, enc_ref, qkv_ref,
    out_w_ref, up_ref, down_ref, dec_ref, copies_ref, tok_ref,
):
    band = lax.axis_index("band")
    bands = lax.axis_size("band")
    offset = offset_ref[...]
    blocks = [embed(ref, tok_ref, enc_ref, offset)[1] for ref in (before_ref, after_ref)]
    queries = heads_ref[0]
    keys = [heads_ref[1]] + [heads_of(mm(n, qkv_ref[:, W : 2 * W])) for n in blocks]
    values = [heads_ref[2]] + [mm(n, qkv_ref[:, 2 * W :]).astype(BF16) for n in blocks]

    q_row = lax.broadcasted_iota(jnp.int32, (TOK, TOK), 0) % 2
    k_row = lax.broadcasted_iota(jnp.int32, (TOK, TOK), 1) % 2
    see_before = (((q_row == 0) | (k_row == 1)) & (band > 0)).astype(F32)
    see_after = (((q_row == 1) | (k_row == 0)) & (band < bands - 1)).astype(F32)
    masks = [None, see_before, see_after]

    attended = []
    for h in range(HEADS):
        at = slice(h * HEAD_DIM, (h + 1) * HEAD_DIM)
        total, mix = 0.0, 0.0
        for n in range(3):
            scores = lax.dot_general(
                queries[:, at], keys[n][:, at], (((1,), (1,)), ((), ())),
                preferred_element_type=F32,
            )
            weights = jnp.exp(scores * SCORE)
            if masks[n] is not None:
                weights = weights * masks[n]
            total = total + jnp.sum(weights, axis=-1, keepdims=True)
            mix = mix + mm(weights.astype(BF16), values[n][:, at])
        attended.append((mix / total).astype(BF16))
    attended = jnp.concatenate(attended, axis=1)

    mixed = embedded_ref[...] + mm(attended, out_w_ref[...])
    hidden = jax.nn.gelu(mm(rms(mixed).astype(BF16), up_ref[...])).astype(BF16)
    mixed = mixed + mm(hidden, down_ref[...])
    last = rms(mixed).astype(BF16)
    dec = jnp.concatenate([dec_ref[...].astype(F32), jnp.zeros((LANES - C, W), F32)], axis=0)
    drift = noise_ref[...] * lax.dot_general(
        last, dec.astype(BF16), (((1,), (1,)), ((), ())), preferred_element_type=F32
    )

    lane = lax.broadcasted_iota(jnp.int32, (SUB, LANES), 1)
    tiles = [0.0] * TILES
    for r in range(GROUP):
        tile, off = divmod(r * C, LANES)
        v = drift[r * SUB : (r + 1) * SUB, :]
        if off:
            v = pltpu.roll(v, off, 1)
        if off + C > LANES:
            tiles[tile] = tiles[tile] + jnp.where(lane >= off, v, 0.0)
            tiles[tile + 1] = tiles[tile + 1] + jnp.where(lane < off, v, 0.0)
        else:
            tiles[tile] = tiles[tile] + v
    packed = jnp.concatenate(tiles, axis=1)
    packed = packed.astype(BF16)
    for i in range(4):
        copies_ref[i] = packed


def middle_kernel(group_ref, sent_ref):
    parts = [group_ref[i].astype(F32) for i in range(4)]
    sent_ref[...] = ((parts[0] + parts[1]) + (parts[2] + parts[3])).astype(BF16)


def base_kernel(group_ref, anchor_ref, states_ref, area_ref, base_ref, old_ref, scale_ref):
    step = lax.axis_index("step")
    band = lax.axis_index("band")
    last = step == lax.axis_size("step") - 1
    place = jnp.where(last, 4, (step + 1) % 4)
    window = jnp.where(place > 0, group_ref[0].astype(F32), 0.0)
    for i in range(1, 4):
        window = window + jnp.where(place > i, group_ref[i].astype(F32), 0.0)
    base_ref[...] = to_packed(anchor_ref[...]) + window
    old_ref[...] = to_packed(states_ref[0])
    row = 2 * band + lax.broadcasted_iota(jnp.int32, (SUB, NLAT), 0) % 2
    pick = lax.broadcasted_iota(jnp.int32, (SUB, NLAT), 1) == row
    area = jnp.sum(jnp.where(pick, area_ref[...], 0.0), axis=1, keepdims=True)
    scale_ref[...] = jnp.broadcast_to(area, scale_ref.shape)


def close_kernel(
    back4_ref, back8_ref, back12_ref, base_ref, old_ref, scale_ref, new_ref, part_ref
):
    new = base_ref[...] + (
        back4_ref[...].astype(F32) + back8_ref[...].astype(F32) + back12_ref[...].astype(F32)
    )
    for g in range(PACKS):
        new_ref[0, :, g * SPAN : (g + 1) * SPAN] = new[2 * g : 2 * g + 2, :]
    miss = new - old_ref[...]
    miss = miss * miss
    part = miss[:, :LANES]
    for t in range(1, TILES):
        part = part + miss[:, t * LANES : (t + 1) * LANES]
    part = jnp.sum(part * scale_ref[...], axis=0, keepdims=True)
    part_ref[...] = jnp.broadcast_to(part, part_ref.shape)


def local_vmem(*arrays):
    return [pltpu.with_memory_space_constraint(a, pltpu.VMEM) for a in arrays]


def in_hbm(*arrays):
    return [pltpu.with_memory_space_constraint(a, pltpu.HBM) for a in arrays]


def local(
    states, anchor, step_index, sigmas, enc_w, noise_embed, qkv_w, out_w, up_w, down_w, dec_w
):
    steps, bands = lax.axis_size("step"), lax.axis_size("band")
    vmem = pl.BlockSpec(memory_space=pltpu.VMEM)
    smem = pl.BlockSpec(memory_space=pltpu.SMEM)
    hbm = pl.BlockSpec(memory_space=pltpu.HBM)

    block = pl.pallas_call(
        open_kernel, out_shape=pltpu.VMEM((SUB, SPAN), BF16), in_specs=[hbm] * 2, out_specs=vmem,
        scratch_shapes=[pltpu.VMEM((2, LON * C), F32)],
        cost_estimate=pl.CostEstimate(flops=10**10, bytes_accessed=10**6, transcendentals=0),
        name="open", compiler_params=pltpu.CompilerParams(vmem_limit_bytes=8 << 20),
    )(*in_hbm(states, anchor))

    index = lax.ppermute(step_index, "step", [((s + 1) % steps, s) for s in range(steps)])
    before = lax.ppermute(block, "band", [(b, b + 1) for b in range(bands - 1)])
    after = lax.ppermute(block, "band", [(b + 1, b) for b in range(bands - 1)])

    def limit(mib):
        return pltpu.CompilerParams(vmem_limit_bytes=mib << 20)

    tokens = pltpu.VMEM((TOK, LANES), F32)
    own = pl.pallas_call(
        own_kernel,
        out_shape=(
            pltpu.VMEM((TOK, W), F32), pltpu.VMEM((3, TOK, W), BF16), pltpu.VMEM((1, W), F32),
            pltpu.VMEM((1, LANES), F32),
        ),
        in_specs=[vmem] * 6, out_specs=(vmem,) * 4, scratch_shapes=[tokens],
        name="own", compiler_params=limit(16),
    )(*local_vmem(index[None], sigmas[None], noise_embed[None], block, enc_w, qkv_w))
    copies = pl.pallas_call(
        denoise_kernel,
        out_shape=pltpu.VMEM((4, SUB, SPAN), BF16),
        in_specs=[vmem] * 12, out_specs=vmem, scratch_shapes=[tokens],
        name="denoise", compiler_params=limit(32),
    )(*local_vmem(before, after, *own, enc_w, qkv_w, out_w, up_w, down_w, dec_w.T))

    group = lax.all_to_all(
        copies, "step", 0, 0, tiled=True,
        axis_index_groups=[[(4 * g + i - 1) % steps for i in range(4)] for g in range(steps // 4)],
    )
    packed = pltpu.VMEM((SUB, SPAN), F32)
    sent = pl.pallas_call(
        middle_kernel, out_shape=pltpu.VMEM((SUB, SPAN), BF16), in_specs=[vmem], out_specs=vmem,
        name="middle", compiler_params=limit(8),
    )(*local_vmem(group))
    far = []
    for pairs in FAR:
        far.append(lax.ppermute(sent, "step", pairs))
    latitude = np.pi * ((np.arange(NLAT, dtype=np.float32) + 0.5) / NLAT - 0.5)
    area = np.cos(latitude).astype(np.float32)
    base = pl.pallas_call(
        base_kernel, out_shape=(packed, packed, pltpu.VMEM((SUB, LANES), F32)),
        in_specs=[vmem] * 4, out_specs=(vmem,) * 3, name="base", compiler_params=limit(8),
    )(*local_vmem(group, anchor, states, jnp.asarray(area)[None]))
    new_states, part = pl.pallas_call(
        close_kernel,
        out_shape=(pltpu.VMEM(states.shape, F32), pltpu.VMEM((bands, LANES), F32)),
        in_specs=[vmem] * 6, out_specs=(vmem, vmem), name="close", compiler_params=limit(8),
    )(*local_vmem(*far, *base))
    parts = lax.all_to_all(part, "band", 0, 0, tiled=True)
    change = jnp.sum(parts)[None] / (np.float32(area.sum()) * (LON * C))
    return new_states, change


def solution(mesh):
    placed = (
        P("step", "band", None), P("band", None), P("step"), P(), P(), P(), P(), P(), P(), P(), P(),
    )
    return jax.shard_map(
        local,
        mesh=mesh,
        in_specs=placed,
        out_specs=(P("step", "band", None), P("step")),
        check_vma=False,
    )
```

```python
import math

import jax
import jax.numpy as jnp
import numpy as np
from jax import lax
from jax.experimental import pallas as pl
from jax.experimental.pallas import tpu as pltpu
from jax.sharding import PartitionSpec as P

C = 84
W = 512
HEADS = 4
HEAD_DIM = 128
LON = 128
NLAT = 64
LEVELS = 20
LANES = 128
GROUP = 32
SPAN = GROUP * C
PACKS = LON // GROUP
SUB = 2 * PACKS
TILES = SPAN // LANES
TOK = 2 * LON

FAR = (
    [(2, 3), (0, 4), (1, 5), (15, 6)] + [(s, s + 4) for s in range(3, 11)] + [(14, 15)],
    [(2, 7), (1, 8), (0, 9), (15, 10), (6, 11), (5, 12), (4, 13), (3, 14), (10, 15)],
    [(15, 11), (0, 12), (1, 13), (2, 14), (3, 15)],
)

epsilon = 1e-06
SCORE = 3.0 / math.sqrt(HEAD_DIM)

F32 = jnp.float32
BF16 = jnp.bfloat16


def rms(v):
    return v * lax.rsqrt(jnp.mean(v * v, axis=-1, keepdims=True) + epsilon)


def mm(a, b):
    return jnp.dot(a, b, preferred_element_type=F32)


def to_packed(rows):
    return jnp.concatenate([rows[:, g * SPAN : (g + 1) * SPAN] for g in range(PACKS)], axis=0)


def sight_kernel(sight_ref):
    band = lax.axis_index("band")
    q_row = lax.broadcasted_iota(jnp.int32, (TOK, TOK), 0) % 2
    k_row = lax.broadcasted_iota(jnp.int32, (TOK, TOK), 1) % 2
    before = ((q_row == 0) | (k_row == 1)) & (band > 0)
    after = ((q_row == 1) | (k_row == 0)) & (band < lax.axis_size("band") - 1)
    sight_ref[0] = before.astype(F32)
    sight_ref[1] = after.astype(F32)


def open_kernel(states_ref, anchor_ref, sight_ref, out_ref):
    last = lax.axis_index("step") == lax.axis_size("step") - 1

    @pl.when(last)
    def _():
        out_ref[...] = to_packed(anchor_ref[...]).astype(BF16)

    @pl.when(jnp.logical_not(last))
    def _():
        out_ref[...] = to_packed(states_ref[0]).astype(BF16)


def unpack_tokens(block_ref, tok_ref):
    lane = lax.broadcasted_iota(jnp.int32, (SUB, LANES), 1)
    x = block_ref[...].astype(F32)
    for r in range(GROUP):
        tile, off = divmod(r * C, LANES)
        v = x[:, tile * LANES : (tile + 1) * LANES]
        if off + C > LANES:
            v = jnp.where(lane >= off, v, x[:, (tile + 1) * LANES : (tile + 2) * LANES])
        if off:
            v = pltpu.roll(v, LANES - off, 1)
        tok_ref[r * SUB : (r + 1) * SUB, :] = v


def embed(ref, tok_ref, enc_ref, offset):
    unpack_tokens(ref, tok_ref)
    enc = jnp.concatenate(
        [enc_ref[...].astype(F32), jnp.zeros((LANES - C, W), F32)], axis=0
    ).astype(BF16)
    embedded = mm(tok_ref[...].astype(BF16), enc) + offset
    return embedded, rms(embedded).astype(BF16)


def heads_of(projected):
    return jnp.concatenate(
        [rms(projected[:, h * HEAD_DIM : (h + 1) * HEAD_DIM]) for h in range(HEADS)], axis=1
    ).astype(BF16)


def attend(queries, keys, values, mask):
    scores = lax.dot_general(
        queries, keys, (((1,), (1,)), ((), ())), preferred_element_type=F32
    )
    weights = jnp.exp(scores * SCORE)
    if mask is not None:
        weights = weights * mask
    return jnp.sum(weights, axis=-1, keepdims=True), mm(weights.astype(BF16), values)


def own_kernel(
    index_ref, sigma_ref, embed_ref, here_ref, enc_ref, qkv_ref, embedded_ref, queries_ref,
    total_ref, mix_ref, offset_ref, noise_ref, tok_ref,
):
    level = lax.broadcasted_iota(jnp.int32, (1, LEVELS), 1)
    noise = jnp.sum(
        jnp.where(level == index_ref[...], sigma_ref[...], 0.0), axis=1, keepdims=True
    )
    offset = jnp.log(noise) * embed_ref[...]
    offset_ref[...] = offset
    noise_ref[...] = jnp.broadcast_to(noise, noise_ref.shape)
    embedded, normed = embed(here_ref, tok_ref, enc_ref, offset)
    embedded_ref[...] = embedded
    queries = heads_of(mm(normed, qkv_ref[:, :W]))
    queries_ref[...] = queries
    keys = heads_of(mm(normed, qkv_ref[:, W : 2 * W]))
    values = mm(normed, qkv_ref[:, 2 * W :]).astype(BF16)
    for h in range(HEADS):
        at = slice(h * HEAD_DIM, (h + 1) * HEAD_DIM)
        total_ref[h], mix_ref[h] = attend(queries[:, at], keys[:, at], values[:, at], None)


def denoise_kernel(
    before_ref, after_ref, embedded_ref, queries_ref, total_ref, mix_ref, offset_ref, noise_ref,
    sight_ref, enc_ref, qkv_ref, out_w_ref, up_ref, down_ref, dec_ref, copies_ref, tok_ref,
):
    offset = offset_ref[...]
    blocks = [embed(ref, tok_ref, enc_ref, offset)[1] for ref in (before_ref, after_ref)]
    queries = queries_ref[...]
    keys = [heads_of(mm(n, qkv_ref[:, W : 2 * W])) for n in blocks]
    values = [mm(n, qkv_ref[:, 2 * W :]).astype(BF16) for n in blocks]

    attended = []
    for h in range(HEADS):
        at = slice(h * HEAD_DIM, (h + 1) * HEAD_DIM)
        total, mix = total_ref[h], mix_ref[h]
        for n in range(2):
            more, part = attend(queries[:, at], keys[n][:, at], values[n][:, at], sight_ref[n])
            total, mix = total + more, mix + part
        attended.append((mix / total).astype(BF16))
    attended = jnp.concatenate(attended, axis=1)

    mixed = embedded_ref[...] + mm(attended, out_w_ref[...])
    hidden = jax.nn.gelu(mm(rms(mixed).astype(BF16), up_ref[...])).astype(BF16)
    mixed = mixed + mm(hidden, down_ref[...])
    last = rms(mixed).astype(BF16)
    dec = jnp.concatenate([dec_ref[...].astype(F32), jnp.zeros((LANES - C, W), F32)], axis=0)
    drift = noise_ref[...] * lax.dot_general(
        last, dec.astype(BF16), (((1,), (1,)), ((), ())), preferred_element_type=F32
    )

    lane = lax.broadcasted_iota(jnp.int32, (SUB, LANES), 1)
    tiles = [0.0] * TILES
    for r in range(GROUP):
        tile, off = divmod(r * C, LANES)
        v = drift[r * SUB : (r + 1) * SUB, :]
        if off:
            v = pltpu.roll(v, off, 1)
        if off + C > LANES:
            tiles[tile] = tiles[tile] + jnp.where(lane >= off, v, 0.0)
            tiles[tile + 1] = tiles[tile + 1] + jnp.where(lane < off, v, 0.0)
        else:
            tiles[tile] = tiles[tile] + v
    packed = jnp.concatenate(tiles, axis=1)
    packed = packed.astype(BF16)
    for i in range(4):
        copies_ref[i] = packed


def middle_kernel(group_ref, sent_ref):
    parts = [group_ref[i].astype(F32) for i in range(4)]
    sent_ref[...] = ((parts[0] + parts[1]) + (parts[2] + parts[3])).astype(BF16)


def base_kernel(group_ref, anchor_ref, states_ref, area_ref, base_ref, old_ref, scale_ref):
    step = lax.axis_index("step")
    band = lax.axis_index("band")
    last = step == lax.axis_size("step") - 1
    place = jnp.where(last, 4, (step + 1) % 4)
    window = jnp.where(place > 0, group_ref[0].astype(F32), 0.0)
    for i in range(1, 4):
        window = window + jnp.where(place > i, group_ref[i].astype(F32), 0.0)
    base_ref[...] = to_packed(anchor_ref[...]) + window
    old_ref[...] = to_packed(states_ref[0])
    row = 2 * band + lax.broadcasted_iota(jnp.int32, (SUB, NLAT), 0) % 2
    pick = lax.broadcasted_iota(jnp.int32, (SUB, NLAT), 1) == row
    area = jnp.sum(jnp.where(pick, area_ref[...], 0.0), axis=1, keepdims=True)
    scale_ref[...] = jnp.broadcast_to(area, scale_ref.shape)


def close_kernel(
    back4_ref, back8_ref, back12_ref, base_ref, old_ref, scale_ref, new_ref, part_ref
):
    new = base_ref[...] + (
        back4_ref[...].astype(F32) + back8_ref[...].astype(F32) + back12_ref[...].astype(F32)
    )
    for g in range(PACKS):
        new_ref[0, :, g * SPAN : (g + 1) * SPAN] = new[2 * g : 2 * g + 2, :]
    miss = new - old_ref[...]
    miss = miss * miss
    part = miss[:, :LANES]
    for t in range(1, TILES):
        part = part + miss[:, t * LANES : (t + 1) * LANES]
    part = jnp.sum(part * scale_ref[...], axis=0, keepdims=True)
    part_ref[...] = jnp.broadcast_to(part, part_ref.shape)


def local_vmem(*arrays):
    return [pltpu.with_memory_space_constraint(a, pltpu.VMEM) for a in arrays]


def local(
    states, anchor, step_index, sigmas, enc_w, noise_embed, qkv_w, out_w, up_w, down_w, dec_w
):
    steps, bands = lax.axis_size("step"), lax.axis_size("band")
    vmem = pl.BlockSpec(memory_space=pltpu.VMEM)
    smem = pl.BlockSpec(memory_space=pltpu.SMEM)
    hbm = pl.BlockSpec(memory_space=pltpu.HBM)

    sight = pl.pallas_call(
        sight_kernel, out_shape=pltpu.VMEM((2, TOK, TOK), F32), out_specs=vmem, name="sight",
        cost_estimate=pl.CostEstimate(flops=10**10, bytes_accessed=10**6, transcendentals=0),
        compiler_params=pltpu.CompilerParams(vmem_limit_bytes=8 << 20),
    )()
    block = pl.pallas_call(
        open_kernel, out_shape=pltpu.VMEM((SUB, SPAN), BF16), in_specs=[vmem] * 3, out_specs=vmem,
        cost_estimate=pl.CostEstimate(flops=10**10, bytes_accessed=10**6, transcendentals=0),
        name="open", compiler_params=pltpu.CompilerParams(vmem_limit_bytes=8 << 20),
    )(*local_vmem(states, anchor, sight))

    index = lax.ppermute(step_index, "step", [((s + 1) % steps, s) for s in range(steps)])
    before = lax.ppermute(block, "band", [(b, b + 1) for b in range(bands - 1)])
    after = lax.ppermute(block, "band", [(b + 1, b) for b in range(bands - 1)])

    def limit(mib):
        return pltpu.CompilerParams(vmem_limit_bytes=mib << 20)

    tokens = pltpu.VMEM((TOK, LANES), F32)
    own = pl.pallas_call(
        own_kernel,
        out_shape=(
            pltpu.VMEM((TOK, W), F32), pltpu.VMEM((TOK, W), BF16),
            pltpu.VMEM((HEADS, TOK, 1), F32), pltpu.VMEM((HEADS, TOK, HEAD_DIM), F32),
            pltpu.VMEM((1, W), F32), pltpu.VMEM((1, LANES), F32),
        ),
        in_specs=[vmem] * 6, out_specs=(vmem,) * 6, scratch_shapes=[tokens],
        name="own", compiler_params=limit(16),
    )(*local_vmem(index[None], sigmas[None], noise_embed[None], block, enc_w, qkv_w))
    copies = pl.pallas_call(
        denoise_kernel,
        out_shape=pltpu.VMEM((4, SUB, SPAN), BF16),
        in_specs=[vmem] * 15, out_specs=vmem, scratch_shapes=[tokens],
        name="denoise", compiler_params=limit(32),
    )(*local_vmem(before, after, *own, sight, enc_w, qkv_w, out_w, up_w, down_w, dec_w.T))

    group = lax.all_to_all(
        copies, "step", 0, 0, tiled=True,
        axis_index_groups=[[(4 * g + i - 1) % steps for i in range(4)] for g in range(steps // 4)],
    )
    packed = pltpu.VMEM((SUB, SPAN), F32)
    sent = pl.pallas_call(
        middle_kernel, out_shape=pltpu.VMEM((SUB, SPAN), BF16), in_specs=[vmem], out_specs=vmem,
        name="middle", compiler_params=limit(8),
    )(*local_vmem(group))
    far = []
    for pairs in FAR:
        far.append(lax.ppermute(sent, "step", pairs))
    latitude = np.pi * ((np.arange(NLAT, dtype=np.float32) + 0.5) / NLAT - 0.5)
    area = np.cos(latitude).astype(np.float32)
    base = pl.pallas_call(
        base_kernel, out_shape=(packed, packed, pltpu.VMEM((SUB, LANES), F32)),
        in_specs=[vmem] * 4, out_specs=(vmem,) * 3, name="base", compiler_params=limit(8),
    )(*local_vmem(group, anchor, states, jnp.asarray(area)[None]))
    new_states, part = pl.pallas_call(
        close_kernel,
        out_shape=(pltpu.VMEM(states.shape, F32), pltpu.VMEM((bands, LANES), F32)),
        in_specs=[vmem] * 6, out_specs=(vmem, vmem), name="close", compiler_params=limit(8),
    )(*local_vmem(*far, *base))
    parts = lax.all_to_all(part, "band", 0, 0, tiled=True)
    change = jnp.sum(parts)[None] / (np.float32(area.sum()) * (LON * C))
    return new_states, change


def solution(mesh):
    placed = (
        P("step", "band", None), P("band", None), P("step"), P(), P(), P(), P(), P(), P(), P(), P(),
    )
    return jax.shard_map(
        local,
        mesh=mesh,
        in_specs=placed,
        out_specs=(P("step", "band", None), P("step")),
        check_vma=False,
    )
```

```python
import math

import jax
import jax.numpy as jnp
import numpy as np
from jax import lax
from jax.experimental import pallas as pl
from jax.experimental.pallas import tpu as pltpu
from jax.sharding import PartitionSpec as P

C = 84
W = 512
HEADS = 4
HEAD_DIM = 128
LON = 128
NLAT = 64
LEVELS = 20
LANES = 128
GROUP = 32
SPAN = GROUP * C
PACKS = LON // GROUP
SUB = 2 * PACKS
TILES = SPAN // LANES
TOK = 2 * LON

NEAR = [(15, 3)] + [(s, s + 4) for s in range(7)]
SKIP = [(2, 7), (1, 8), (0, 9), (15, 10), (14, 15)]
NEXT = [(s, s + 4) for s in range(7, 11)]
PAIR = [(6, 11), (5, 12), (4, 13), (3, 14), (10, 15)]

epsilon = 1e-06
SCORE = 3.0 / math.sqrt(HEAD_DIM)

F32 = jnp.float32
BF16 = jnp.bfloat16


def rms(v):
    return v * lax.rsqrt(jnp.mean(v * v, axis=-1, keepdims=True) + epsilon)


def mm(a, b):
    return jnp.dot(a, b, preferred_element_type=F32)


def to_packed(rows):
    return jnp.concatenate([rows[:, g * SPAN : (g + 1) * SPAN] for g in range(PACKS)], axis=0)


def sight_kernel(sight_ref):
    band = lax.axis_index("band")
    q_row = lax.broadcasted_iota(jnp.int32, (TOK, TOK), 0) % 2
    k_row = lax.broadcasted_iota(jnp.int32, (TOK, TOK), 1) % 2
    before = ((q_row == 0) | (k_row == 1)) & (band > 0)
    after = ((q_row == 1) | (k_row == 0)) & (band < lax.axis_size("band") - 1)
    sight_ref[0] = before.astype(F32)
    sight_ref[1] = after.astype(F32)


def open_kernel(states_ref, anchor_ref, sight_ref, out_ref):
    last = lax.axis_index("step") == lax.axis_size("step") - 1

    @pl.when(last)
    def _():
        out_ref[...] = to_packed(anchor_ref[...]).astype(BF16)

    @pl.when(jnp.logical_not(last))
    def _():
        out_ref[...] = to_packed(states_ref[0]).astype(BF16)


def unpack_tokens(block_ref, tok_ref):
    lane = lax.broadcasted_iota(jnp.int32, (SUB, LANES), 1)
    x = block_ref[...].astype(F32)
    for r in range(GROUP):
        tile, off = divmod(r * C, LANES)
        v = x[:, tile * LANES : (tile + 1) * LANES]
        if off + C > LANES:
            v = jnp.where(lane >= off, v, x[:, (tile + 1) * LANES : (tile + 2) * LANES])
        if off:
            v = pltpu.roll(v, LANES - off, 1)
        tok_ref[r * SUB : (r + 1) * SUB, :] = v


def embed(ref, tok_ref, enc_ref, offset):
    unpack_tokens(ref, tok_ref)
    enc = jnp.concatenate(
        [enc_ref[...].astype(F32), jnp.zeros((LANES - C, W), F32)], axis=0
    ).astype(BF16)
    embedded = mm(tok_ref[...].astype(BF16), enc) + offset
    return embedded, rms(embedded).astype(BF16)


def heads_of(projected):
    return jnp.concatenate(
        [rms(projected[:, h * HEAD_DIM : (h + 1) * HEAD_DIM]) for h in range(HEADS)], axis=1
    ).astype(BF16)


def attend(queries, keys, values, mask):
    scores = lax.dot_general(
        queries, keys, (((1,), (1,)), ((), ())), preferred_element_type=F32
    )
    weights = jnp.exp(scores * SCORE)
    if mask is not None:
        weights = weights * mask
    return jnp.sum(weights, axis=-1, keepdims=True), mm(weights.astype(BF16), values)


def own_kernel(
    index_ref, sigma_ref, embed_ref, here_ref, enc_ref, qkv_ref, embedded_ref, queries_ref,
    total_ref, mix_ref, offset_ref, noise_ref, tok_ref,
):
    level = lax.broadcasted_iota(jnp.int32, (1, LEVELS), 1)
    noise = jnp.sum(
        jnp.where(level == index_ref[...], sigma_ref[...], 0.0), axis=1, keepdims=True
    )
    offset = jnp.log(noise) * embed_ref[...]
    offset_ref[...] = offset
    noise_ref[...] = jnp.broadcast_to(noise, noise_ref.shape)
    embedded, normed = embed(here_ref, tok_ref, enc_ref, offset)
    embedded_ref[...] = embedded
    queries = heads_of(mm(normed, qkv_ref[:, :W]))
    queries_ref[...] = queries
    keys = heads_of(mm(normed, qkv_ref[:, W : 2 * W]))
    values = mm(normed, qkv_ref[:, 2 * W :]).astype(BF16)
    for h in range(HEADS):
        at = slice(h * HEAD_DIM, (h + 1) * HEAD_DIM)
        total_ref[h], mix_ref[h] = attend(queries[:, at], keys[:, at], values[:, at], None)


def denoise_kernel(
    before_ref, after_ref, embedded_ref, queries_ref, total_ref, mix_ref, offset_ref, noise_ref,
    sight_ref, enc_ref, qkv_ref, out_w_ref, up_ref, down_ref, dec_ref, copies_ref, tok_ref,
):
    offset = offset_ref[...]
    blocks = [embed(ref, tok_ref, enc_ref, offset)[1] for ref in (before_ref, after_ref)]
    queries = queries_ref[...]
    keys = [heads_of(mm(n, qkv_ref[:, W : 2 * W])) for n in blocks]
    values = [mm(n, qkv_ref[:, 2 * W :]).astype(BF16) for n in blocks]

    attended = []
    for h in range(HEADS):
        at = slice(h * HEAD_DIM, (h + 1) * HEAD_DIM)
        total, mix = total_ref[h], mix_ref[h]
        for n in range(2):
            more, part = attend(queries[:, at], keys[n][:, at], values[n][:, at], sight_ref[n])
            total, mix = total + more, mix + part
        attended.append((mix / total).astype(BF16))
    attended = jnp.concatenate(attended, axis=1)

    mixed = embedded_ref[...] + mm(attended, out_w_ref[...])
    hidden = jax.nn.gelu(mm(rms(mixed).astype(BF16), up_ref[...])).astype(BF16)
    mixed = mixed + mm(hidden, down_ref[...])
    last = rms(mixed).astype(BF16)
    dec = jnp.concatenate([dec_ref[...].astype(F32), jnp.zeros((LANES - C, W), F32)], axis=0)
    drift = noise_ref[...] * lax.dot_general(
        last, dec.astype(BF16), (((1,), (1,)), ((), ())), preferred_element_type=F32
    )

    lane = lax.broadcasted_iota(jnp.int32, (SUB, LANES), 1)
    tiles = [0.0] * TILES
    for r in range(GROUP):
        tile, off = divmod(r * C, LANES)
        v = drift[r * SUB : (r + 1) * SUB, :]
        if off:
            v = pltpu.roll(v, off, 1)
        if off + C > LANES:
            tiles[tile] = tiles[tile] + jnp.where(lane >= off, v, 0.0)
            tiles[tile + 1] = tiles[tile + 1] + jnp.where(lane < off, v, 0.0)
        else:
            tiles[tile] = tiles[tile] + v
    packed = jnp.concatenate(tiles, axis=1)
    packed = packed.astype(BF16)
    for i in range(4):
        copies_ref[i] = packed


def middle_kernel(group_ref, sent_ref):
    parts = [group_ref[i].astype(F32) for i in range(4)]
    sent_ref[...] = ((parts[0] + parts[1]) + (parts[2] + parts[3])).astype(BF16)


def both_kernel(sent_ref, near_ref, both_ref):
    both_ref[...] = (sent_ref[...].astype(F32) + near_ref[...].astype(F32)).astype(BF16)


def base_kernel(group_ref, anchor_ref, states_ref, area_ref, base_ref, old_ref, scale_ref):
    step = lax.axis_index("step")
    band = lax.axis_index("band")
    last = step == lax.axis_size("step") - 1
    place = jnp.where(last, 4, (step + 1) % 4)
    window = jnp.where(place > 0, group_ref[0].astype(F32), 0.0)
    for i in range(1, 4):
        window = window + jnp.where(place > i, group_ref[i].astype(F32), 0.0)
    base_ref[...] = to_packed(anchor_ref[...]) + window
    old_ref[...] = to_packed(states_ref[0])
    row = 2 * band + lax.broadcasted_iota(jnp.int32, (SUB, NLAT), 0) % 2
    pick = lax.broadcasted_iota(jnp.int32, (SUB, NLAT), 1) == row
    area = jnp.sum(jnp.where(pick, area_ref[...], 0.0), axis=1, keepdims=True)
    scale_ref[...] = jnp.broadcast_to(area, scale_ref.shape)


def close_kernel(
    near_ref, skip_ref, next_ref, pair_ref, base_ref, old_ref, scale_ref, new_ref, part_ref
):
    new = base_ref[...] + (
        (near_ref[...].astype(F32) + next_ref[...].astype(F32))
        + (skip_ref[...].astype(F32) + pair_ref[...].astype(F32))
    )
    for g in range(PACKS):
        new_ref[0, :, g * SPAN : (g + 1) * SPAN] = new[2 * g : 2 * g + 2, :]
    miss = new - old_ref[...]
    miss = miss * miss
    part = miss[:, :LANES]
    for t in range(1, TILES):
        part = part + miss[:, t * LANES : (t + 1) * LANES]
    part = jnp.sum(part * scale_ref[...], axis=0, keepdims=True)
    part_ref[...] = jnp.broadcast_to(part, part_ref.shape)


def local_vmem(*arrays):
    return [pltpu.with_memory_space_constraint(a, pltpu.VMEM) for a in arrays]


def local(
    states, anchor, step_index, sigmas, enc_w, noise_embed, qkv_w, out_w, up_w, down_w, dec_w
):
    steps, bands = lax.axis_size("step"), lax.axis_size("band")
    vmem = pl.BlockSpec(memory_space=pltpu.VMEM)
    smem = pl.BlockSpec(memory_space=pltpu.SMEM)
    hbm = pl.BlockSpec(memory_space=pltpu.HBM)

    sight = pl.pallas_call(
        sight_kernel, out_shape=pltpu.VMEM((2, TOK, TOK), F32), out_specs=vmem, name="sight",
        cost_estimate=pl.CostEstimate(flops=10**10, bytes_accessed=10**6, transcendentals=0),
        compiler_params=pltpu.CompilerParams(vmem_limit_bytes=8 << 20),
    )()
    block = pl.pallas_call(
        open_kernel, out_shape=pltpu.VMEM((SUB, SPAN), BF16), in_specs=[vmem] * 3, out_specs=vmem,
        cost_estimate=pl.CostEstimate(flops=10**10, bytes_accessed=10**6, transcendentals=0),
        name="open", compiler_params=pltpu.CompilerParams(vmem_limit_bytes=8 << 20),
    )(*local_vmem(states, anchor, sight))

    index = lax.ppermute(step_index, "step", [((s + 1) % steps, s) for s in range(steps)])
    before = lax.ppermute(block, "band", [(b, b + 1) for b in range(bands - 1)])
    after = lax.ppermute(block, "band", [(b + 1, b) for b in range(bands - 1)])

    def limit(mib):
        return pltpu.CompilerParams(vmem_limit_bytes=mib << 20)

    tokens = pltpu.VMEM((TOK, LANES), F32)
    own = pl.pallas_call(
        own_kernel,
        out_shape=(
            pltpu.VMEM((TOK, W), F32), pltpu.VMEM((TOK, W), BF16),
            pltpu.VMEM((HEADS, TOK, 1), F32), pltpu.VMEM((HEADS, TOK, HEAD_DIM), F32),
            pltpu.VMEM((1, W), F32), pltpu.VMEM((1, LANES), F32),
        ),
        in_specs=[vmem] * 6, out_specs=(vmem,) * 6, scratch_shapes=[tokens],
        name="own", compiler_params=limit(16),
    )(*local_vmem(index[None], sigmas[None], noise_embed[None], block, enc_w, qkv_w))
    copies = pl.pallas_call(
        denoise_kernel,
        out_shape=pltpu.VMEM((4, SUB, SPAN), BF16),
        in_specs=[vmem] * 15, out_specs=vmem, scratch_shapes=[tokens],
        name="denoise", compiler_params=limit(32),
    )(*local_vmem(before, after, *own, sight, enc_w, qkv_w, out_w, up_w, down_w, dec_w.T))

    group = lax.all_to_all(
        copies, "step", 0, 0, tiled=True,
        axis_index_groups=[[(4 * g + i - 1) % steps for i in range(4)] for g in range(steps // 4)],
    )
    packed = pltpu.VMEM((SUB, SPAN), F32)
    sent = pl.pallas_call(
        middle_kernel, out_shape=pltpu.VMEM((SUB, SPAN), BF16), in_specs=[vmem], out_specs=vmem,
        name="middle", compiler_params=limit(8),
    )(*local_vmem(group))

    def moved(array, pairs):
        return lax.ppermute(array, "step", pairs)

    near = moved(sent, NEAR)
    skip = moved(sent, SKIP)
    following = moved(sent, NEXT)
    both = pl.pallas_call(
        both_kernel, out_shape=pltpu.VMEM((SUB, SPAN), BF16), in_specs=[vmem] * 2, out_specs=vmem,
        name="both", compiler_params=limit(8),
    )(*local_vmem(sent, near))
    pair = moved(both, PAIR)
    far = (near, skip, following, pair)
    latitude = np.pi * ((np.arange(NLAT, dtype=np.float32) + 0.5) / NLAT - 0.5)
    area = np.cos(latitude).astype(np.float32)
    base = pl.pallas_call(
        base_kernel, out_shape=(packed, packed, pltpu.VMEM((SUB, LANES), F32)),
        in_specs=[vmem] * 4, out_specs=(vmem,) * 3, name="base", compiler_params=limit(8),
    )(*local_vmem(group, anchor, states, jnp.asarray(area)[None]))
    new_states, part = pl.pallas_call(
        close_kernel,
        out_shape=(pltpu.VMEM(states.shape, F32), pltpu.VMEM((bands, LANES), F32)),
        in_specs=[vmem] * 7, out_specs=(vmem, vmem), name="close", compiler_params=limit(8),
    )(*local_vmem(*far, *base))
    parts = lax.all_to_all(part, "band", 0, 0, tiled=True)
    change = jnp.sum(parts)[None] / (np.float32(area.sum()) * (LON * C))
    return new_states, change


def solution(mesh):
    placed = (
        P("step", "band", None), P("band", None), P("step"), P(), P(), P(), P(), P(), P(), P(), P(),
    )
    return jax.shard_map(
        local,
        mesh=mesh,
        in_specs=placed,
        out_specs=(P("step", "band", None), P("step")),
        check_vma=False,
    )
```

```python
import math

import jax
import jax.numpy as jnp
import numpy as np
from jax import lax
from jax.experimental import pallas as pl
from jax.experimental.pallas import tpu as pltpu
from jax.sharding import PartitionSpec as P

C = 84
W = 512
HEADS = 4
HEAD_DIM = 128
LON = 128
NLAT = 64
LEVELS = 20
LANES = 128
GROUP = 32
SPAN = GROUP * C
PACKS = LON // GROUP
SUB = 2 * PACKS
TILES = SPAN // LANES
TOK = 2 * LON

NEAR = [(15, 3)] + [(s, s + 4) for s in range(7)]
SKIP = [(2, 7), (1, 8), (0, 9), (15, 10), (14, 15)]
NEXT = [(s, s + 4) for s in range(7, 11)]
PAIR = [(6, 11), (5, 12), (4, 13), (3, 14), (10, 15)]

epsilon = 1e-06
SCORE = 3.0 / math.sqrt(HEAD_DIM)

F32 = jnp.float32
BF16 = jnp.bfloat16


def rms(v):
    return v * lax.rsqrt(jnp.mean(v * v, axis=-1, keepdims=True) + epsilon)


def mm(a, b):
    return jnp.dot(a, b, preferred_element_type=F32)


def to_packed(rows):
    return jnp.concatenate([rows[:, g * SPAN : (g + 1) * SPAN] for g in range(PACKS)], axis=0)


def sight_kernel(sight_ref):
    band = lax.axis_index("band")
    q_row = lax.broadcasted_iota(jnp.int32, (TOK, TOK), 0) % 2
    k_row = lax.broadcasted_iota(jnp.int32, (TOK, TOK), 1) % 2
    before = ((q_row == 0) | (k_row == 1)) & (band > 0)
    after = ((q_row == 1) | (k_row == 0)) & (band < lax.axis_size("band") - 1)
    sight_ref[0] = before.astype(F32)
    sight_ref[1] = after.astype(F32)


def open_kernel(states_ref, anchor_ref, sight_ref, out_ref):
    last = lax.axis_index("step") == lax.axis_size("step") - 1

    @pl.when(last)
    def _():
        out_ref[...] = to_packed(anchor_ref[...]).astype(BF16)

    @pl.when(jnp.logical_not(last))
    def _():
        out_ref[...] = to_packed(states_ref[0]).astype(BF16)


def unpack_tokens(block_ref, tok_ref):
    lane = lax.broadcasted_iota(jnp.int32, (SUB, LANES), 1)
    x = block_ref[...].astype(F32)
    for r in range(GROUP):
        tile, off = divmod(r * C, LANES)
        v = x[:, tile * LANES : (tile + 1) * LANES]
        if off + C > LANES:
            v = jnp.where(lane >= off, v, x[:, (tile + 1) * LANES : (tile + 2) * LANES])
        if off:
            v = pltpu.roll(v, LANES - off, 1)
        tok_ref[r * SUB : (r + 1) * SUB, :] = v


def embed(ref, tok_ref, enc_ref, offset):
    unpack_tokens(ref, tok_ref)
    enc = jnp.concatenate(
        [enc_ref[...].astype(F32), jnp.zeros((LANES - C, W), F32)], axis=0
    ).astype(BF16)
    embedded = mm(tok_ref[...].astype(BF16), enc) + offset
    return embedded, rms(embedded).astype(BF16)


def heads_of(projected):
    return jnp.concatenate(
        [rms(projected[:, h * HEAD_DIM : (h + 1) * HEAD_DIM]) for h in range(HEADS)], axis=1
    ).astype(BF16)


def attend(queries, keys, values, mask):
    scores = lax.dot_general(
        queries, keys, (((1,), (1,)), ((), ())), preferred_element_type=F32
    )
    weights = jnp.exp(scores * SCORE)
    if mask is not None:
        weights = weights * mask
    return jnp.sum(weights, axis=-1, keepdims=True), mm(weights.astype(BF16), values)


def own_kernel(
    index_ref, sigma_ref, embed_ref, here_ref, enc_ref, qkv_ref, embedded_ref, queries_ref,
    total_ref, mix_ref, offset_ref, noise_ref, tok_ref,
):
    level = lax.broadcasted_iota(jnp.int32, (1, LEVELS), 1)
    noise = jnp.sum(
        jnp.where(level == index_ref[...], sigma_ref[...], 0.0), axis=1, keepdims=True
    )
    offset = jnp.log(noise) * embed_ref[...]
    offset_ref[...] = offset
    noise_ref[...] = jnp.broadcast_to(noise, noise_ref.shape)
    embedded, normed = embed(here_ref, tok_ref, enc_ref, offset)
    embedded_ref[...] = embedded
    queries = heads_of(mm(normed, qkv_ref[:, :W]))
    queries_ref[...] = queries
    keys = heads_of(mm(normed, qkv_ref[:, W : 2 * W]))
    values = mm(normed, qkv_ref[:, 2 * W :]).astype(BF16)
    for h in range(HEADS):
        at = slice(h * HEAD_DIM, (h + 1) * HEAD_DIM)
        total_ref[h], mix_ref[h] = attend(queries[:, at], keys[:, at], values[:, at], None)


def denoise_kernel(
    before_ref, after_ref, embedded_ref, queries_ref, total_ref, mix_ref, offset_ref, noise_ref,
    sight_ref, enc_ref, qkv_ref, out_w_ref, up_ref, down_ref, dec_ref, copies_ref, tok_ref,
):
    offset = offset_ref[...]
    blocks = [embed(ref, tok_ref, enc_ref, offset)[1] for ref in (before_ref, after_ref)]
    queries = queries_ref[...]
    keys = [heads_of(mm(n, qkv_ref[:, W : 2 * W])) for n in blocks]
    values = [mm(n, qkv_ref[:, 2 * W :]).astype(BF16) for n in blocks]

    attended = []
    for h in range(HEADS):
        at = slice(h * HEAD_DIM, (h + 1) * HEAD_DIM)
        total, mix = total_ref[h], mix_ref[h]
        for n in range(2):
            more, part = attend(queries[:, at], keys[n][:, at], values[n][:, at], sight_ref[n])
            total, mix = total + more, mix + part
        attended.append((mix / total).astype(BF16))
    attended = jnp.concatenate(attended, axis=1)

    mixed = embedded_ref[...] + mm(attended, out_w_ref[...])
    hidden = jax.nn.gelu(mm(rms(mixed).astype(BF16), up_ref[...])).astype(BF16)
    mixed = mixed + mm(hidden, down_ref[...])
    last = rms(mixed).astype(BF16)
    dec = jnp.concatenate([dec_ref[...].astype(F32), jnp.zeros((LANES - C, W), F32)], axis=0)
    drift = noise_ref[...] * lax.dot_general(
        last, dec.astype(BF16), (((1,), (1,)), ((), ())), preferred_element_type=F32
    )

    lane = lax.broadcasted_iota(jnp.int32, (SUB, LANES), 1)
    tiles = [0.0] * TILES
    for r in range(GROUP):
        tile, off = divmod(r * C, LANES)
        v = drift[r * SUB : (r + 1) * SUB, :]
        if off:
            v = pltpu.roll(v, off, 1)
        if off + C > LANES:
            tiles[tile] = tiles[tile] + jnp.where(lane >= off, v, 0.0)
            tiles[tile + 1] = tiles[tile + 1] + jnp.where(lane < off, v, 0.0)
        else:
            tiles[tile] = tiles[tile] + v
    packed = jnp.concatenate(tiles, axis=1)
    packed = packed.astype(BF16)
    for i in range(4):
        copies_ref[i] = packed


def middle_kernel(group_ref, sent_ref, total_ref):
    parts = [group_ref[i].astype(F32) for i in range(4)]
    total = (parts[0] + parts[1]) + (parts[2] + parts[3])
    total_ref[...] = total
    sent_ref[...] = total.astype(BF16)


def both_kernel(total_ref, near_ref, both_ref):
    both_ref[...] = total_ref[...] + near_ref[...].astype(F32)


def base_kernel(group_ref, anchor_ref, states_ref, area_ref, base_ref, old_ref, scale_ref):
    step = lax.axis_index("step")
    band = lax.axis_index("band")
    last = step == lax.axis_size("step") - 1
    place = jnp.where(last, 4, (step + 1) % 4)
    window = jnp.where(place > 0, group_ref[0].astype(F32), 0.0)
    for i in range(1, 4):
        window = window + jnp.where(place > i, group_ref[i].astype(F32), 0.0)
    base_ref[...] = to_packed(anchor_ref[...]) + window
    old_ref[...] = to_packed(states_ref[0])
    row = 2 * band + lax.broadcasted_iota(jnp.int32, (SUB, NLAT), 0) % 2
    pick = lax.broadcasted_iota(jnp.int32, (SUB, NLAT), 1) == row
    area = jnp.sum(jnp.where(pick, area_ref[...], 0.0), axis=1, keepdims=True)
    scale_ref[...] = jnp.broadcast_to(area, scale_ref.shape)


def close_kernel(
    near_ref, skip_ref, next_ref, pair_ref, base_ref, old_ref, scale_ref, new_ref, part_ref
):
    new = base_ref[...] + (
        (near_ref[...].astype(F32) + next_ref[...].astype(F32))
        + (skip_ref[...].astype(F32) + pair_ref[...])
    )
    for g in range(PACKS):
        new_ref[0, :, g * SPAN : (g + 1) * SPAN] = new[2 * g : 2 * g + 2, :]
    miss = new - old_ref[...]
    miss = miss * miss
    part = miss[:, :LANES]
    for t in range(1, TILES):
        part = part + miss[:, t * LANES : (t + 1) * LANES]
    part = jnp.sum(part * scale_ref[...], axis=0, keepdims=True)
    part_ref[...] = jnp.broadcast_to(part, part_ref.shape)


def local_vmem(*arrays):
    return [pltpu.with_memory_space_constraint(a, pltpu.VMEM) for a in arrays]


def local(
    states, anchor, step_index, sigmas, enc_w, noise_embed, qkv_w, out_w, up_w, down_w, dec_w
):
    steps, bands = lax.axis_size("step"), lax.axis_size("band")
    vmem = pl.BlockSpec(memory_space=pltpu.VMEM)
    smem = pl.BlockSpec(memory_space=pltpu.SMEM)
    hbm = pl.BlockSpec(memory_space=pltpu.HBM)

    sight = pl.pallas_call(
        sight_kernel, out_shape=pltpu.VMEM((2, TOK, TOK), F32), out_specs=vmem, name="sight",
        cost_estimate=pl.CostEstimate(flops=10**10, bytes_accessed=10**6, transcendentals=0),
        compiler_params=pltpu.CompilerParams(vmem_limit_bytes=8 << 20),
    )()
    block = pl.pallas_call(
        open_kernel, out_shape=pltpu.VMEM((SUB, SPAN), BF16), in_specs=[vmem] * 3, out_specs=vmem,
        cost_estimate=pl.CostEstimate(flops=10**10, bytes_accessed=10**6, transcendentals=0),
        name="open", compiler_params=pltpu.CompilerParams(vmem_limit_bytes=8 << 20),
    )(*local_vmem(states, anchor, sight))

    index = lax.ppermute(step_index, "step", [((s + 1) % steps, s) for s in range(steps)])
    before = lax.ppermute(block, "band", [(b, b + 1) for b in range(bands - 1)])
    after = lax.ppermute(block, "band", [(b + 1, b) for b in range(bands - 1)])

    def limit(mib):
        return pltpu.CompilerParams(vmem_limit_bytes=mib << 20)

    tokens = pltpu.VMEM((TOK, LANES), F32)
    own = pl.pallas_call(
        own_kernel,
        out_shape=(
            pltpu.VMEM((TOK, W), F32), pltpu.VMEM((TOK, W), BF16),
            pltpu.VMEM((HEADS, TOK, 1), F32), pltpu.VMEM((HEADS, TOK, HEAD_DIM), F32),
            pltpu.VMEM((1, W), F32), pltpu.VMEM((1, LANES), F32),
        ),
        in_specs=[vmem] * 6, out_specs=(vmem,) * 6, scratch_shapes=[tokens],
        name="own", compiler_params=limit(16),
    )(*local_vmem(index[None], sigmas[None], noise_embed[None], block, enc_w, qkv_w))
    copies = pl.pallas_call(
        denoise_kernel,
        out_shape=pltpu.VMEM((4, SUB, SPAN), BF16),
        in_specs=[vmem] * 15, out_specs=vmem, scratch_shapes=[tokens],
        name="denoise", compiler_params=limit(32),
    )(*local_vmem(before, after, *own, sight, enc_w, qkv_w, out_w, up_w, down_w, dec_w.T))

    group = lax.all_to_all(
        copies, "step", 0, 0, tiled=True,
        axis_index_groups=[[(4 * g + i - 1) % steps for i in range(4)] for g in range(steps // 4)],
    )
    packed = pltpu.VMEM((SUB, SPAN), F32)
    sent, total = pl.pallas_call(
        middle_kernel, out_shape=(pltpu.VMEM((SUB, SPAN), BF16), packed), in_specs=[vmem],
        out_specs=(vmem, vmem),
        name="middle", compiler_params=limit(8),
    )(*local_vmem(group))

    def moved(array, pairs):
        return lax.ppermute(array, "step", pairs)

    near = moved(sent, NEAR)
    skip = moved(sent, SKIP)
    following = moved(sent, NEXT)
    both = pl.pallas_call(
        both_kernel, out_shape=packed, in_specs=[vmem] * 2, out_specs=vmem,
        name="both", compiler_params=limit(8),
    )(*local_vmem(total, near))
    pair = moved(both, PAIR)
    far = (near, skip, following, pair)
    latitude = np.pi * ((np.arange(NLAT, dtype=np.float32) + 0.5) / NLAT - 0.5)
    area = np.cos(latitude).astype(np.float32)
    base = pl.pallas_call(
        base_kernel, out_shape=(packed, packed, pltpu.VMEM((SUB, LANES), F32)),
        in_specs=[vmem] * 4, out_specs=(vmem,) * 3, name="base", compiler_params=limit(8),
    )(*local_vmem(group, anchor, states, jnp.asarray(area)[None]))
    new_states, part = pl.pallas_call(
        close_kernel,
        out_shape=(pltpu.VMEM(states.shape, F32), pltpu.VMEM((bands, LANES), F32)),
        in_specs=[vmem] * 7, out_specs=(vmem, vmem), name="close", compiler_params=limit(8),
    )(*local_vmem(*far, *base))
    parts = lax.all_to_all(part, "band", 0, 0, tiled=True)
    change = jnp.sum(parts)[None] / (np.float32(area.sum()) * (LON * C))
    return new_states, change


def solution(mesh):
    placed = (
        P("step", "band", None), P("band", None), P("step"), P(), P(), P(), P(), P(), P(), P(), P(),
    )
    return jax.shard_map(
        local,
        mesh=mesh,
        in_specs=placed,
        out_specs=(P("step", "band", None), P("step")),
        check_vma=False,
    )
```

```python
import math

import jax
import jax.numpy as jnp
import numpy as np
from jax import lax
from jax.experimental import pallas as pl
from jax.experimental.pallas import tpu as pltpu
from jax.sharding import PartitionSpec as P

C = 84
W = 512
HEADS = 4
HEAD_DIM = 128
LON = 128
NLAT = 64
LEVELS = 20
LANES = 128
GROUP = 32
SPAN = GROUP * C
PACKS = LON // GROUP
SUB = 2 * PACKS
TILES = SPAN // LANES
TOK = 2 * LON

NEAR = [(15, 3)] + [(s, s + 4) for s in range(7)]
SKIP = [(2, 7), (1, 8), (0, 9), (15, 10), (14, 15)]
NEXT = [(s, s + 4) for s in range(7, 11)]
PAIR = [(6, 11), (5, 12), (4, 13), (3, 14), (10, 15)]

epsilon = 1e-06
SCORE = 3.0 / math.sqrt(HEAD_DIM)

F32 = jnp.float32
BF16 = jnp.bfloat16


def rms(v):
    return v * lax.rsqrt(jnp.mean(v * v, axis=-1, keepdims=True) + epsilon)


def mm(a, b):
    return jnp.dot(a, b, preferred_element_type=F32)


def to_packed(rows):
    return jnp.concatenate([rows[:, g * SPAN : (g + 1) * SPAN] for g in range(PACKS)], axis=0)


def sight_kernel(sight_ref):
    band = lax.axis_index("band")
    q_row = lax.broadcasted_iota(jnp.int32, (TOK, TOK), 0) % 2
    k_row = lax.broadcasted_iota(jnp.int32, (TOK, TOK), 1) % 2
    before = ((q_row == 0) | (k_row == 1)) & (band > 0)
    after = ((q_row == 1) | (k_row == 0)) & (band < lax.axis_size("band") - 1)
    sight_ref[0] = before.astype(F32)
    sight_ref[1] = after.astype(F32)


def open_kernel(states_ref, anchor_ref, sight_ref, out_ref):
    last = lax.axis_index("step") == lax.axis_size("step") - 1

    @pl.when(last)
    def _():
        out_ref[...] = to_packed(anchor_ref[...]).astype(BF16)

    @pl.when(jnp.logical_not(last))
    def _():
        out_ref[...] = to_packed(states_ref[0]).astype(BF16)


def unpack_tokens(block_ref, tok_ref):
    lane = lax.broadcasted_iota(jnp.int32, (SUB, LANES), 1)
    x = block_ref[...].astype(F32)
    for r in range(GROUP):
        tile, off = divmod(r * C, LANES)
        v = x[:, tile * LANES : (tile + 1) * LANES]
        if off + C > LANES:
            v = jnp.where(lane >= off, v, x[:, (tile + 1) * LANES : (tile + 2) * LANES])
        if off:
            v = pltpu.roll(v, LANES - off, 1)
        tok_ref[r * SUB : (r + 1) * SUB, :] = v


def embed(ref, tok_ref, enc_ref, offset):
    unpack_tokens(ref, tok_ref)
    enc = jnp.concatenate(
        [enc_ref[...].astype(F32), jnp.zeros((LANES - C, W), F32)], axis=0
    ).astype(BF16)
    embedded = mm(tok_ref[...].astype(BF16), enc) + offset
    return embedded, rms(embedded).astype(BF16)


def heads_of(projected):
    return jnp.concatenate(
        [rms(projected[:, h * HEAD_DIM : (h + 1) * HEAD_DIM]) for h in range(HEADS)], axis=1
    ).astype(BF16)


def attend(queries, keys, values, mask):
    scores = lax.dot_general(
        queries, keys, (((1,), (1,)), ((), ())), preferred_element_type=F32
    )
    weights = jnp.exp(scores * SCORE)
    if mask is not None:
        weights = weights * mask
    return jnp.sum(weights, axis=-1, keepdims=True), mm(weights.astype(BF16), values)


def own_kernel(
    index_ref, sigma_ref, embed_ref, here_ref, enc_ref, qkv_ref, embedded_ref, queries_ref,
    total_ref, mix_ref, offset_ref, noise_ref, tok_ref,
):
    level = lax.broadcasted_iota(jnp.int32, (1, LEVELS), 1)
    noise = jnp.sum(
        jnp.where(level == index_ref[...], sigma_ref[...], 0.0), axis=1, keepdims=True
    )
    offset = jnp.log(noise) * embed_ref[...]
    offset_ref[...] = offset
    noise_ref[...] = jnp.broadcast_to(noise, noise_ref.shape)
    embedded, normed = embed(here_ref, tok_ref, enc_ref, offset)
    embedded_ref[...] = embedded
    queries = heads_of(mm(normed, qkv_ref[:, :W]))
    queries_ref[...] = queries
    keys = heads_of(mm(normed, qkv_ref[:, W : 2 * W]))
    values = mm(normed, qkv_ref[:, 2 * W :]).astype(BF16)
    for h in range(HEADS):
        at = slice(h * HEAD_DIM, (h + 1) * HEAD_DIM)
        total_ref[h], mix_ref[h] = attend(queries[:, at], keys[:, at], values[:, at], None)


def denoise_kernel(
    before_ref, after_ref, embedded_ref, queries_ref, total_ref, mix_ref, offset_ref, noise_ref,
    sight_ref, enc_ref, qkv_ref, out_w_ref, up_ref, down_ref, dec_ref, copies_ref, tok_ref,
):
    offset = offset_ref[...]
    blocks = [embed(ref, tok_ref, enc_ref, offset)[1] for ref in (before_ref, after_ref)]
    queries = queries_ref[...]
    keys = [heads_of(mm(n, qkv_ref[:, W : 2 * W])) for n in blocks]
    values = [mm(n, qkv_ref[:, 2 * W :]).astype(BF16) for n in blocks]

    attended = []
    for h in range(HEADS):
        at = slice(h * HEAD_DIM, (h + 1) * HEAD_DIM)
        total, mix = total_ref[h], mix_ref[h]
        for n in range(2):
            more, part = attend(queries[:, at], keys[n][:, at], values[n][:, at], sight_ref[n])
            total, mix = total + more, mix + part
        attended.append((mix / total).astype(BF16))
    attended = jnp.concatenate(attended, axis=1)

    mixed = embedded_ref[...] + mm(attended, out_w_ref[...])
    hidden = jax.nn.gelu(mm(rms(mixed).astype(BF16), up_ref[...])).astype(BF16)
    mixed = mixed + mm(hidden, down_ref[...])
    last = rms(mixed).astype(BF16)
    dec = jnp.concatenate([dec_ref[...].astype(F32), jnp.zeros((LANES - C, W), F32)], axis=0)
    drift = noise_ref[...] * lax.dot_general(
        last, dec.astype(BF16), (((1,), (1,)), ((), ())), preferred_element_type=F32
    )

    lane = lax.broadcasted_iota(jnp.int32, (SUB, LANES), 1)
    tiles = [0.0] * TILES
    for r in range(GROUP):
        tile, off = divmod(r * C, LANES)
        v = drift[r * SUB : (r + 1) * SUB, :]
        if off:
            v = pltpu.roll(v, off, 1)
        if off + C > LANES:
            tiles[tile] = tiles[tile] + jnp.where(lane >= off, v, 0.0)
            tiles[tile + 1] = tiles[tile + 1] + jnp.where(lane < off, v, 0.0)
        else:
            tiles[tile] = tiles[tile] + v
    packed = jnp.concatenate(tiles, axis=1)
    packed = packed.astype(BF16)
    for i in range(4):
        copies_ref[i] = packed


def middle_kernel(group_ref, sent_ref, total_ref):
    parts = [group_ref[i].astype(F32) for i in range(4)]
    total = (parts[0] + parts[1]) + (parts[2] + parts[3])
    total_ref[...] = total
    sent_ref[...] = total.astype(BF16)


def both_kernel(total_ref, near_ref, both_ref):
    both_ref[...] = (total_ref[...] + near_ref[...].astype(F32)).astype(BF16)


def base_kernel(group_ref, anchor_ref, states_ref, area_ref, base_ref, old_ref, scale_ref):
    step = lax.axis_index("step")
    band = lax.axis_index("band")
    last = step == lax.axis_size("step") - 1
    place = jnp.where(last, 4, (step + 1) % 4)
    window = jnp.where(place > 0, group_ref[0].astype(F32), 0.0)
    for i in range(1, 4):
        window = window + jnp.where(place > i, group_ref[i].astype(F32), 0.0)
    base_ref[...] = to_packed(anchor_ref[...]) + window
    old_ref[...] = to_packed(states_ref[0])
    row = 2 * band + lax.broadcasted_iota(jnp.int32, (SUB, NLAT), 0) % 2
    pick = lax.broadcasted_iota(jnp.int32, (SUB, NLAT), 1) == row
    area = jnp.sum(jnp.where(pick, area_ref[...], 0.0), axis=1, keepdims=True)
    scale_ref[...] = jnp.broadcast_to(area, scale_ref.shape)


def close_kernel(
    near_ref, skip_ref, next_ref, pair_ref, base_ref, old_ref, scale_ref, new_ref, part_ref
):
    new = base_ref[...] + (
        (near_ref[...].astype(F32) + next_ref[...].astype(F32))
        + (skip_ref[...].astype(F32) + pair_ref[...].astype(F32))
    )
    for g in range(PACKS):
        new_ref[0, :, g * SPAN : (g + 1) * SPAN] = new[2 * g : 2 * g + 2, :]
    miss = new - old_ref[...]
    miss = miss * miss
    part = miss[:, :LANES]
    for t in range(1, TILES):
        part = part + miss[:, t * LANES : (t + 1) * LANES]
    part = jnp.sum(part * scale_ref[...], axis=0, keepdims=True)
    part_ref[...] = jnp.broadcast_to(part, part_ref.shape)


def local_vmem(*arrays):
    return [pltpu.with_memory_space_constraint(a, pltpu.VMEM) for a in arrays]


def local(
    states, anchor, step_index, sigmas, enc_w, noise_embed, qkv_w, out_w, up_w, down_w, dec_w
):
    steps, bands = lax.axis_size("step"), lax.axis_size("band")
    vmem = pl.BlockSpec(memory_space=pltpu.VMEM)
    smem = pl.BlockSpec(memory_space=pltpu.SMEM)
    hbm = pl.BlockSpec(memory_space=pltpu.HBM)

    sight = pl.pallas_call(
        sight_kernel, out_shape=pltpu.VMEM((2, TOK, TOK), F32), out_specs=vmem, name="sight",
        cost_estimate=pl.CostEstimate(flops=10**10, bytes_accessed=10**6, transcendentals=0),
        compiler_params=pltpu.CompilerParams(vmem_limit_bytes=8 << 20),
    )()
    block = pl.pallas_call(
        open_kernel, out_shape=pltpu.VMEM((SUB, SPAN), BF16), in_specs=[vmem] * 3, out_specs=vmem,
        cost_estimate=pl.CostEstimate(flops=10**10, bytes_accessed=10**6, transcendentals=0),
        name="open", compiler_params=pltpu.CompilerParams(vmem_limit_bytes=8 << 20),
    )(*local_vmem(states, anchor, sight))

    index = lax.ppermute(step_index, "step", [((s + 1) % steps, s) for s in range(steps)])
    before = lax.ppermute(block, "band", [(b, b + 1) for b in range(bands - 1)])
    after = lax.ppermute(block, "band", [(b + 1, b) for b in range(bands - 1)])

    def limit(mib):
        return pltpu.CompilerParams(vmem_limit_bytes=mib << 20)

    tokens = pltpu.VMEM((TOK, LANES), F32)
    own = pl.pallas_call(
        own_kernel,
        out_shape=(
            pltpu.VMEM((TOK, W), F32), pltpu.VMEM((TOK, W), BF16),
            pltpu.VMEM((HEADS, TOK, 1), F32), pltpu.VMEM((HEADS, TOK, HEAD_DIM), F32),
            pltpu.VMEM((1, W), F32), pltpu.VMEM((1, LANES), F32),
        ),
        in_specs=[vmem] * 6, out_specs=(vmem,) * 6, scratch_shapes=[tokens],
        name="own", compiler_params=limit(16),
    )(*local_vmem(index[None], sigmas[None], noise_embed[None], block, enc_w, qkv_w))
    copies = pl.pallas_call(
        denoise_kernel,
        out_shape=pltpu.VMEM((4, SUB, SPAN), BF16),
        in_specs=[vmem] * 15, out_specs=vmem, scratch_shapes=[tokens],
        name="denoise", compiler_params=limit(32),
    )(*local_vmem(before, after, *own, sight, enc_w, qkv_w, out_w, up_w, down_w, dec_w.T))

    group = lax.all_to_all(
        copies, "step", 0, 0, tiled=True,
        axis_index_groups=[[(4 * g + i - 1) % steps for i in range(4)] for g in range(steps // 4)],
    )
    packed = pltpu.VMEM((SUB, SPAN), F32)
    sent, total = pl.pallas_call(
        middle_kernel, out_shape=(pltpu.VMEM((SUB, SPAN), BF16), packed), in_specs=[vmem],
        out_specs=(vmem, vmem),
        name="middle", compiler_params=limit(8),
    )(*local_vmem(group))

    def moved(array, pairs):
        return lax.ppermute(array, "step", pairs)

    near = moved(sent, NEAR)
    skip = moved(sent, SKIP)
    following = moved(sent, NEXT)
    both = pl.pallas_call(
        both_kernel, out_shape=pltpu.VMEM((SUB, SPAN), BF16), in_specs=[vmem] * 2, out_specs=vmem,
        name="both", compiler_params=limit(8),
    )(*local_vmem(total, near))
    pair = moved(both, PAIR)
    far = (near, skip, following, pair)
    latitude = np.pi * ((np.arange(NLAT, dtype=np.float32) + 0.5) / NLAT - 0.5)
    area = np.cos(latitude).astype(np.float32)
    base = pl.pallas_call(
        base_kernel, out_shape=(packed, packed, pltpu.VMEM((SUB, LANES), F32)),
        in_specs=[vmem] * 4, out_specs=(vmem,) * 3, name="base", compiler_params=limit(8),
    )(*local_vmem(group, anchor, states, jnp.asarray(area)[None]))
    new_states, part = pl.pallas_call(
        close_kernel,
        out_shape=(pltpu.VMEM(states.shape, F32), pltpu.VMEM((bands, LANES), F32)),
        in_specs=[vmem] * 7, out_specs=(vmem, vmem), name="close", compiler_params=limit(8),
    )(*local_vmem(*far, *base))
    parts = lax.all_to_all(part, "band", 0, 0, tiled=True)
    change = jnp.sum(parts)[None] / (np.float32(area.sum()) * (LON * C))
    return new_states, change


def solution(mesh):
    placed = (
        P("step", "band", None), P("band", None), P("step"), P(), P(), P(), P(), P(), P(), P(), P(),
    )
    return jax.shard_map(
        local,
        mesh=mesh,
        in_specs=placed,
        out_specs=(P("step", "band", None), P("step")),
        check_vma=False,
    )
```
